256 devices in a mesh: dp: 8 (over y, x_hi), head: 32 (over z, x_lo, core).
Axes of the slice: x: 4 (x_hi: 2, x_lo: 2; x = x_hi * 2 + x_lo), y: 4, z: 8, core: 2. Of those that a mesh axis runs over, the one named last changes fastest.
Arguments:
- query_latent: bfloat16 [2048, 1536], P('dp'), may hold values from -384 to 384
- kv_latent: bfloat16 [2048, 576], P('dp'), may hold values from -48 to 48
- out_grad: bfloat16 [2048, 16384], P('dp', 'head'), may hold values from -20 to 20
- query_up: bfloat16 [1536, 24576], P(None, 'head'), may hold values from -1 to 1
- key_up: bfloat16 [512, 16384], P(None, 'head'), may hold values from -0.25 to 0.25
- value_up: bfloat16 [512, 16384], P(None, 'head'), may hold values from -0.25 to 0.25
Outputs:
- query_latent_grad: float32 [2048, 1536], P(('dp', 'head'))
- kv_latent_grad: float32 [2048, 576], P(('dp', 'head'))
- query_up_grad: bfloat16 [1536, 24576], P(None, 'head')
- key_up_grad: bfloat16 [512, 16384], P(None, 'head')
- value_up_grad: bfloat16 [512, 16384], P(None, 'head')
The draws below stay inside these ranges and needn't reach their ends.
All inputs are finite; a program needn't handle non-finite values.
Results may differ from the reference program's by a relative error of at most 0.035.
Values may be sent and summed in bfloat16 or wider, within the bound.
A program may use at most 64 MiB of HBM per device.

```python
import math
import jax
import jax.numpy as jnp
from jax import lax

QL = 1536
KL = 512
DN = 128
DR = 64
HD_DEV = 4
LENGTH = 256
HEADS = 128
ROWS = 2048
N_DP = 8
N_HEAD = 32


def base_field(key, shape):
    return jnp.clip(jax.random.normal(key, shape, jnp.float32), -6.0, 6.0)


def up_weights(key):
    weight_key = jax.random.fold_in(key, 202)
    raw_field = base_field(weight_key, (QL, HEADS * (DN + DR)))
    weights = (raw_field / math.sqrt(QL)).astype(jnp.bfloat16).astype(jnp.float32)
    return weights


def draw_query_up(key, part):
    return up_weights(key).astype(jnp.bfloat16)


def draw_out_grad(key, part):
    grad_key = jax.random.fold_in(key, 505)
    raw_field = base_field(grad_key, (ROWS, HEADS * DN))
    head_index = (jnp.arange(HEADS * DN, dtype=jnp.int32) // DN).astype(jnp.float32)
    rise = math.sqrt(10.0)
    gain = rise ** (head_index / max(HEADS - 1, 1))
    return (raw_field * gain[None, :]).astype(jnp.bfloat16)


def draw_query_latent(key, part):
    latent_key = jax.random.fold_in(key, 303)
    raw_field = base_field(latent_key, (ROWS, QL))
    return raw_field.astype(jnp.bfloat16)


def draw_kv_latent(key, part):
    kv_key = jax.random.fold_in(key, 404)
    raw_field = base_field(kv_key, (ROWS, KL + DR))
    return raw_field.astype(jnp.bfloat16)


def shard_levels(key, shape, pieces, least, largest):
    level = 1.0
    for position, blocks in pieces:
        heights = jax.random.uniform(jax.random.fold_in(jax.random.fold_in(key, 6), position), (blocks,), jnp.float32, least / len(pieces), largest / len(pieces))
        level = level * jnp.repeat(jnp.exp(heights), shape[position] // blocks).reshape((-1,) + (1,) * (len(shape) - 1 - position))
    return level


def scatter_about(key, shape, scale, reach, cuts=(), kind=jnp.bfloat16):
    values = scale * jax.random.normal(key, shape, jnp.float32)
    if cuts:
        values = values * shard_levels(key, shape, cuts, -0.22, 0.18)
    return jnp.clip(values, -reach, reach).astype(kind)


def setup_inputs(seed: int = 0) -> dict:
    arg_keys = jax.random.split(jax.random.key(seed), 7)
    query_latent = draw_query_latent(jax.random.fold_in(arg_keys[6], 71), 0)
    kv_latent = draw_kv_latent(jax.random.fold_in(arg_keys[6], 71), 0)
    out_grad = draw_out_grad(jax.random.fold_in(arg_keys[6], 71), 0)
    query_up = draw_query_up(jax.random.fold_in(arg_keys[6], 71), 0)
    key_up = scatter_about(arg_keys[4], (KL, HEADS * DN), KL ** -0.5, 0.25, ((1, 32),))
    value_up = scatter_about(arg_keys[5], (KL, HEADS * DN), KL ** -0.5, 0.25, ((1, 32),))
    return {"query_latent": query_latent, "kv_latent": kv_latent, "out_grad": out_grad, "query_up": query_up, "key_up": key_up, "value_up": value_up}


max_rms = 1.0
eps = 1e-06

def rotate(values, length):
    half = values.shape[-1] // 2
    freqs = 10000.0 ** (-2.0 * jnp.arange(half, dtype=jnp.float32) / values.shape[-1])
    angle = jnp.arange(length, dtype=jnp.float32)[:, None] * freqs[None, :]
    cosine = jnp.cos(angle)[:, None, :]
    sine = jnp.sin(angle)[:, None, :]
    first = values[..., :half]
    second = values[..., half:]
    return jnp.concatenate([first * cosine - second * sine, second * cosine + first * sine], axis=-1)

def attend(q_plain, q_rot, keys, key_rot, values):
    length = q_plain.shape[0]
    q_rope = rotate(q_rot.astype(jnp.float32), length).astype(jnp.bfloat16)
    scale = 1.0 / (q_plain.shape[-1] + q_rot.shape[-1]) ** 0.5
    scores = jnp.einsum('shd,thd->hst', q_plain, keys, preferred_element_type=jnp.float32)
    scores = scores + jnp.einsum('shd,thd->hst', q_rope, key_rot, preferred_element_type=jnp.float32)
    scores = scores * scale
    positions = jnp.arange(length)
    allowed = positions[None, :] <= positions[:, None]
    scores = jnp.where(allowed[None], scores, -jnp.inf)
    top = lax.stop_gradient(lax.optimization_barrier(jnp.max(scores, axis=-1, keepdims=True)))
    weights = jnp.exp(scores - top)
    probs = (weights / lax.optimization_barrier(jnp.sum(weights, axis=-1, keepdims=True))).astype(jnp.bfloat16)
    return jnp.einsum('hst,thd->shd', probs, values, preferred_element_type=jnp.float32)

def local_grads(query_latent, kv_latent, out_grad, query_up, key_up, value_up):
    length = query_latent.shape[0]
    heads = key_up.shape[1] // DN
    queries = jnp.dot(query_latent, query_up, preferred_element_type=jnp.float32).astype(jnp.bfloat16)
    queries = queries.reshape(length, heads, DN + DR)
    plain_latent = kv_latent[:, :KL]
    keys = jnp.dot(plain_latent, key_up, preferred_element_type=jnp.float32).astype(jnp.bfloat16).reshape(length, heads, DN)
    values = jnp.dot(plain_latent, value_up, preferred_element_type=jnp.float32).astype(jnp.bfloat16).reshape(length, heads, DN)
    key_rot = jnp.broadcast_to(kv_latent[:, None, KL:], (length, heads, DR))
    attn, pull = jax.vjp(attend, queries[..., :DN], queries[..., DN:], keys, key_rot, values)
    grad_plain, grad_rot, key_grad, rot_grad, value_grad = pull(out_grad.reshape(length, heads, DN).astype(jnp.float32))
    q_grad = jnp.concatenate([grad_plain, grad_rot], axis=-1).reshape(length, heads * (DN + DR))
    rot_sum = lax.optimization_barrier(jnp.sum(rot_grad.astype(jnp.float32), axis=1))
    return (q_grad, key_grad.reshape(length, heads * DN), value_grad.reshape(length, heads * DN), rot_sum)

def transposed(left, right):
    return lax.dot_general(left, right, (((1,), (1,)), ((), ())), preferred_element_type=jnp.float32)

def reference(query_latent, kv_latent, out_grad, query_up, key_up, value_up):
    width_q = HD_DEV * (DN + DR)
    width_k = HD_DEV * DN
    wq_blocks = query_up.reshape(QL, N_HEAD, width_q).transpose(1, 0, 2)
    wk_blocks = key_up.reshape(KL, N_HEAD, width_k).transpose(1, 0, 2)
    wv_blocks = value_up.reshape(KL, N_HEAD, width_k).transpose(1, 0, 2)
    cq_groups = query_latent.reshape(N_DP, LENGTH, QL)
    kv_groups = kv_latent.reshape(N_DP, LENGTH, KL + DR)
    do_groups = out_grad.reshape(N_DP, LENGTH, N_HEAD, width_k).transpose(0, 2, 1, 3)

    def per_group(carry, xs):
        cq_g, kv_g, do_g = xs

        def per_block(block_xs):
            wq_h, wk_h, wv_h, do_h = block_xs
            q_grad, key_grad, value_grad, rot_sum = local_grads(cq_g, kv_g, do_h, wq_h, wk_h, wv_h)
            plain_latent = kv_g[:, :KL]
            grad_wq = jnp.dot(cq_g.T, q_grad, preferred_element_type=jnp.float32)
            grad_wk = jnp.dot(plain_latent.T, key_grad, preferred_element_type=jnp.float32)
            grad_wv = jnp.dot(plain_latent.T, value_grad, preferred_element_type=jnp.float32)
            term_q = transposed(q_grad, wq_h)
            term_kv = transposed(key_grad, wk_h) + transposed(value_grad, wv_h)
            return (grad_wq, grad_wk, grad_wv, term_q, term_kv, rot_sum)
        grad_wq, grad_wk, grad_wv, term_q, term_kv, rot_sum = lax.map(per_block, (wq_blocks, wk_blocks, wv_blocks, do_g))
        carry = (carry[0] + grad_wq, carry[1] + grad_wk, carry[2] + grad_wv)
        latent_q = lax.optimization_barrier(jnp.sum(term_q, axis=0))
        latent_kv = jnp.concatenate([lax.optimization_barrier(jnp.sum(term_kv, axis=0)), lax.optimization_barrier(jnp.sum(rot_sum, axis=0))], axis=1)
        return (carry, (latent_q, latent_kv))
    start = (jnp.zeros((N_HEAD, QL, width_q), jnp.float32), jnp.zeros((N_HEAD, KL, width_k), jnp.float32), jnp.zeros((N_HEAD, KL, width_k), jnp.float32))
    sums, latents = lax.scan(per_group, start, (cq_groups, kv_groups, do_groups))
    grad_wq = sums[0].transpose(1, 0, 2).reshape(QL, N_HEAD * width_q)
    grad_wk = sums[1].transpose(1, 0, 2).reshape(KL, N_HEAD * width_k)
    grad_wv = sums[2].transpose(1, 0, 2).reshape(KL, N_HEAD * width_k)
    total = jnp.sum(grad_wq * grad_wq) + jnp.sum(grad_wk * grad_wk) + jnp.sum(grad_wv * grad_wv)
    count = QL * N_HEAD * width_q + 2 * KL * N_HEAD * width_k
    factor = jnp.minimum(1.0, max_rms * count ** 0.5 / jnp.sqrt(total + eps))
    query_latent_grad = latents[0].reshape(ROWS, QL)
    kv_latent_grad = latents[1].reshape(ROWS, KL + DR)
    return (query_latent_grad, kv_latent_grad, (grad_wq * factor).astype(jnp.bfloat16), (grad_wk * factor).astype(jnp.bfloat16), (grad_wv * factor).astype(jnp.bfloat16))
```

```python
import functools

import jax
import jax.numpy as jnp
from jax import lax
from jax.experimental import pallas as pl
from jax.experimental.pallas import tpu as pltpu
from jax.sharding import PartitionSpec as P

QL = 1536
KL = 512
DN = 128
DR = 64
LAT = 2176

max_rms = 1.0
eps = 1e-06

MESH = pl.DeviceIdType.MESH
BF = jnp.bfloat16
F32 = jnp.float32

PART_ROWS = (768, 768, 512)
PART_COLS = (768, 768, 1024)
ORDERS = ("ABX", "BXA", "XAB")
CHUNK = 32


def rotate(values, length):
    half = values.shape[-1] // 2
    freqs = 10000.0 ** (-2.0 * jnp.arange(half, dtype=jnp.float32) / values.shape[-1])
    angle = jnp.arange(length, dtype=jnp.float32)[:, None] * freqs[None, :]
    cosine = jnp.cos(angle)[:, None, :]
    sine = jnp.sin(angle)[:, None, :]
    first = values[..., :half]
    second = values[..., half:]
    return jnp.concatenate(
        [first * cosine - second * sine, second * cosine + first * sine], axis=-1
    )


def attend(q_plain, q_rot, keys, key_rot, values):
    length = q_plain.shape[0]
    q_rope = rotate(q_rot.astype(jnp.float32), length).astype(jnp.bfloat16)
    scale = 1.0 / (q_plain.shape[-1] + q_rot.shape[-1]) ** 0.5
    scores = jnp.einsum("shd,thd->hst", q_plain, keys, preferred_element_type=jnp.float32)
    scores = scores + jnp.einsum(
        "shd,thd->hst", q_rope, key_rot, preferred_element_type=jnp.float32
    )
    scores = scores * scale
    positions = jnp.arange(length)
    allowed = positions[None, :] <= positions[:, None]
    scores = jnp.where(allowed[None], scores, -jnp.inf)
    top = lax.stop_gradient(jnp.max(scores, axis=-1, keepdims=True))
    weights = jnp.exp(scores - top)
    probs = (weights / jnp.sum(weights, axis=-1, keepdims=True)).astype(jnp.bfloat16)
    return jnp.einsum("hst,thd->shd", probs, values, preferred_element_type=jnp.float32)


def transposed(left, right):
    return lax.dot_general(
        left, right, (((1,), (1,)), ((), ())), preferred_element_type=jnp.float32
    )


def for_rows(rows, step, body):
    def one(i, carry):
        body(pl.multiple_of(i * step, step))
        return carry

    lax.fori_loop(0, rows // step, one, 0)


def places():
    d, h = lax.axis_index("dp"), lax.axis_index("head")
    y, xh = d // 2, d % 2
    b, y0 = y // 2, y % 2
    a = (y0 + b) % 2
    z, r = h // 4, h % 4
    xl, c = r // 2, r % 2
    bits = {"A": a, "B": b, "X": xh}
    peer = {
        "A": (2 * (y + 1 - 2 * y0) + xh, h),
        "B": (2 * (3 - y) + xh, h),
        "X": (2 * y + 1 - xh, h),
        "C": (d, h + 1 - 2 * c),
        "L": (d, h + 2 - 4 * xl),
    }
    for k in range(1, 8):
        peer["Z%d" % k] = (d, (h + 4 * k) % 32)
    return bits, peer, z, xl, c


def greet(peer):
    barrier = pltpu.get_barrier_semaphore()
    for where in peer.values():
        pl.semaphore_signal(barrier, inc=1, device_id=where, device_id_type=MESH)
    pl.semaphore_wait(barrier, len(peer))


def comm_kernel(
    q_ref, kv_ref, lat_ref,
    gq_out, gkv_out, s_out, lat_out,
    stg0, rcv0, redA0, redB0,
    stg1, rcv1, redA1, redB1,
    stg2, rcv2, redA2, redB2,
    gq, gkv,
    lrecv, lsum, zs, zr, lx, lxr,
    sv, sr, sz,
    rs_send, rs_recv, ag_send, ag_recv, l_send, l_recv, s_send, s_recv, out_sem,
):
    bits, peer, z, xl, c = places()
    greet(peer)

    def remote(src, dst, send, recv, where):
        copy = pltpu.make_async_remote_copy(
            src_ref=src, dst_ref=dst, send_sem=send, recv_sem=recv,
            device_id=peer[where], device_id_type=MESH,
        )
        copy.start()
        return copy

    stages = ((stg0, rcv0, redA0, redB0), (stg1, rcv1, redA1, redB1), (stg2, rcv2, redA2, redB2))

    def term(p, lo, n):
        if p == 2:
            return kv_ref[pl.ds(lo, n), :]
        return q_ref[pl.ds(768 * p + lo, n), :]

    def where_rows(p, s):
        rows = PART_ROWS[p]
        return (0, rows // 2, rows // 2 + rows // 4)[s], rows >> (s + 1)

    def source(p, s, lo, n):
        if s == 0:
            return term(p, lo, n)
        return stages[p][1 + s][pl.ds(lo, n), :]

    def rs_start(p, s):
        stg, rcv = stages[p][:2]
        off, n = where_rows(p, s)
        dim = ORDERS[p][s]
        away = (1 - bits[dim]) * n

        def body(i):
            stg[pl.ds(off + i, CHUNK), :] = source(p, s, away + i, CHUNK).astype(BF)

        for_rows(n, CHUNK, body)
        return remote(
            stg.at[pl.ds(off, n)], rcv.at[pl.ds(off, n)],
            rs_send.at[p, s], rs_recv.at[p, s], dim,
        )

    def rs_add(p, s):
        rcv = stages[p][1]
        off, n = where_rows(p, s)
        keep = bits[ORDERS[p][s]] * n
        red = stages[p][2 + s]

        def body(i):
            red[pl.ds(i, CHUNK), :] = source(p, s, keep + i, CHUNK) + rcv[
                pl.ds(off + i, CHUNK), :
            ].astype(F32)

        for_rows(n, CHUNK, body)

    def owned(p, s):
        rows = PART_ROWS[p]
        lo = 0
        for t in range(s + 1):
            lo = lo + bits[ORDERS[p][t]] * (rows >> (t + 1))
        return lo

    def gathered(p, lo, n):
        lo = pl.multiple_of(lo, 32)
        if p == 2:
            return gkv.at[pl.ds(lo, n)]
        return gq.at[pl.ds(768 * p + lo, n)]

    def ag_start(p, s):
        lo, n = owned(p, s), PART_ROWS[p] >> (s + 1)
        block = gathered(p, lo, n)
        return remote(block, block, ag_send.at[p, s], ag_recv.at[p, s], ORDERS[p][s])

    first = [rs_start(p, 0) for p in (2, 0, 1)]
    core = remote(lat_ref.at[:, 1 - c], lrecv, l_send.at[0], l_recv.at[0], "C")
    core.wait()

    def core_body(k, carry):
        lsum[k] = lat_ref[k, c] + lrecv[k]
        return carry

    lax.fori_loop(0, 16, core_body, 0)

    def zs_body(k, carry):
        zs[k] = jnp.concatenate([lsum[2 * k], lsum[2 * k + 1]], axis=0).astype(BF)
        return carry

    lax.fori_loop(0, 8, zs_body, 0)
    zcopies = [
        remote(zs.at[(z + k) % 8], zr.at[k - 1], l_send.at[k], l_recv.at[k], "Z%d" % k)
        for k in range(1, 8)
    ]
    for copy in first:
        copy.wait()
    second = []
    for p in (2, 0, 1):
        rs_add(p, 0)
        second.append(rs_start(p, 1))
    third = []
    for copy, p in zip(second, (2, 0, 1)):
        copy.wait()
        rs_add(p, 1)
        third.append(rs_start(p, 2))
    for copy in zcopies:
        copy.wait()
    lx[0] = lsum[2 * z]
    lx[1] = lsum[2 * z + 1]
    for k in range(7):
        got = zr[k].astype(F32)
        lx[0] = lx[0] + got[:8]
        lx[1] = lx[1] + got[8:]
    xcopy = remote(lx.at[1 - xl], lxr, l_send.at[8], l_recv.at[8], "L")
    sv[0] = jnp.zeros((8, 128), F32)
    for copy, p in zip(third, (2, 0, 1)):
        copy.wait()
        off, n = where_rows(p, 2)
        keep = bits[ORDERS[p][2]] * n
        lo = owned(p, 2)
        rcv, red = stages[p][1], stages[p][3]
        target = gkv if p == 2 else gq
        base = 0 if p == 2 else 768 * p

        def body(i):
            total = red[pl.ds(keep + i, CHUNK), :] + rcv[pl.ds(off + i, CHUNK), :].astype(F32)
            target[pl.ds(pl.multiple_of(base + lo + i, CHUNK), CHUNK), :] = total.astype(BF)
            square = total * total
            part = square[:, :128]
            for j in range(1, PART_COLS[p] // 128):
                part = part + square[:, 128 * j : 128 * (j + 1)]
            sv[0] = sv[0] + part[:8] + part[8:16] + part[16:24] + part[24:32]

        for_rows(n, CHUNK, body)

    def s_step(i, dim):
        return remote(sv.at[i], sr.at[i], s_send.at[i], s_recv.at[i], dim)

    def s_add(copy, i):
        copy.wait()
        sv[i + 1] = sv[i] + sr[i]

    s0 = s_step(0, "A")
    gather = [ag_start(p, 2) for p in (2, 0, 1)]
    s_add(s0, 0)
    s1 = s_step(1, "C")
    xcopy.wait()
    lat_out[...] = lx[xl] + lxr[...]
    s_add(s1, 1)
    s2 = s_step(2, "B")
    later = []
    for copy, p in zip(gather, (2, 0, 1)):
        copy.wait()
        later.append(ag_start(p, 1))
    s_add(s2, 2)
    s3 = s_step(3, "L")
    s_add(s3, 3)
    s4 = s_step(4, "X")
    last = []
    for copy, p in zip(later, (2, 0, 1)):
        copy.wait()
        last.append(ag_start(p, 0))
    s_add(s4, 4)
    szc = [
        remote(sv.at[5], sz.at[z], s_send.at[4 + k], s_recv.at[4 + k], "Z%d" % k)
        for k in range(1, 8)
    ]
    sz[z] = sv[5]
    for copy in szc:
        copy.wait()
    s_out[...] = sz[...]
    outs = []
    for i, (copy, p) in enumerate(zip(last, (2, 0, 1))):
        copy.wait()
        if p == 2:
            out = pltpu.make_async_copy(gkv, gkv_out, out_sem.at[p])
        else:
            out = pltpu.make_async_copy(
                gq.at[pl.ds(768 * p, 768)], gq_out.at[pl.ds(768 * p, 768)], out_sem.at[p]
            )
        out.start()
        outs.append(out)
    for out in outs:
        out.wait()


def communicate(dwq, dwkv, lat):
    scratch = []
    for rows, cols in zip(PART_ROWS, PART_COLS):
        moved = rows // 2 + rows // 4 + rows // 8
        scratch += [
            pltpu.VMEM((moved, cols), BF),
            pltpu.VMEM((moved, cols), BF),
            pltpu.VMEM((rows // 2, cols), F32),
            pltpu.VMEM((rows // 4, cols), F32),
        ]
    scratch += [
        pltpu.VMEM((1536, 768), BF),
        pltpu.VMEM((512, 1024), BF),
        pltpu.VMEM((16, 8, LAT), F32),
        pltpu.VMEM((16, 8, LAT), F32),
        pltpu.VMEM((8, 16, LAT), BF),
        pltpu.VMEM((7, 16, LAT), BF),
        pltpu.VMEM((2, 8, LAT), F32),
        pltpu.VMEM((8, LAT), F32),
        pltpu.VMEM((6, 8, 128), F32),
        pltpu.VMEM((5, 8, 128), F32),
        pltpu.VMEM((8, 8, 128), F32),
        pltpu.SemaphoreType.DMA((3, 3)),
        pltpu.SemaphoreType.DMA((3, 3)),
        pltpu.SemaphoreType.DMA((3, 3)),
        pltpu.SemaphoreType.DMA((3, 3)),
        pltpu.SemaphoreType.DMA((9,)),
        pltpu.SemaphoreType.DMA((9,)),
        pltpu.SemaphoreType.DMA((12,)),
        pltpu.SemaphoreType.DMA((12,)),
        pltpu.SemaphoreType.DMA((3,)),
    ]
    vmem = pl.BlockSpec(memory_space=pltpu.VMEM)
    hbm = pl.BlockSpec(memory_space=pl.ANY)
    return pl.pallas_call(
        comm_kernel,
        out_shape=(
            jax.ShapeDtypeStruct((1536, 768), BF),
            jax.ShapeDtypeStruct((512, 1024), BF),
            jax.ShapeDtypeStruct((8, 8, 128), F32),
            jax.ShapeDtypeStruct((8, LAT), F32),
        ),
        in_specs=[vmem] * 3,
        out_specs=(hbm, hbm, vmem, vmem),
        scratch_shapes=scratch,
        name="comm",
        compiler_params=pltpu.CompilerParams(
            collective_id=0, has_side_effects=True, vmem_limit_bytes=50 << 20
        ),
    )(dwq, dwkv, lat.reshape(16, 2, 8, LAT))


def finish_kernel(count, s_ref, lat_ref, q_ref, kv_ref, ql_out, kvl_out, q_out, k_out, v_out):
    total = jnp.sum(s_ref[...], axis=0)
    total = jnp.sum(total, axis=0, keepdims=True)
    total = jnp.sum(total, axis=1, keepdims=True)
    factor = jnp.minimum(1.0, max_rms * count**0.5 / jnp.sqrt(total + eps))
    q_out[...] = (q_ref[...].astype(F32) * factor).astype(BF)
    k_out[...] = (kv_ref[:, :512].astype(F32) * factor).astype(BF)
    v_out[...] = (kv_ref[:, 512:].astype(F32) * factor).astype(BF)

    @pl.when(pl.program_id(0) == 0)
    def _():
        ql_out[...] = lat_ref[:, :QL]
        kvl_out[...] = lat_ref[:, QL : QL + KL + DR]


def finish(count, s, lat, gq, gkv):
    steps = 4
    return pl.pallas_call(
        functools.partial(finish_kernel, count),
        grid=(steps,),
        out_shape=(
            jax.ShapeDtypeStruct((8, QL), F32),
            jax.ShapeDtypeStruct((8, KL + DR), F32),
            jax.ShapeDtypeStruct((1536, 768), BF),
            jax.ShapeDtypeStruct((512, 512), BF),
            jax.ShapeDtypeStruct((512, 512), BF),
        ),
        in_specs=[
            pl.BlockSpec((8, 8, 128), lambda i: (0, 0, 0)),
            pl.BlockSpec((8, LAT), lambda i: (0, 0)),
            pl.BlockSpec((1536 // steps, 768), lambda i: (i, 0)),
            pl.BlockSpec((512 // steps, 1024), lambda i: (i, 0)),
        ],
        out_specs=(
            pl.BlockSpec((8, QL), lambda i: (0, 0)),
            pl.BlockSpec((8, KL + DR), lambda i: (0, 0)),
            pl.BlockSpec((1536 // steps, 768), lambda i: (i, 0)),
            pl.BlockSpec((512 // steps, 512), lambda i: (i, 0)),
            pl.BlockSpec((512 // steps, 512), lambda i: (i, 0)),
        ),
        name="finish",
    )(s, lat, gq, gkv)


def per_device(query_latent, kv_latent, out_grad, query_up, key_up, value_up):
    length = query_latent.shape[0]
    heads = key_up.shape[1] // DN
    queries = jnp.dot(query_latent, query_up, preferred_element_type=F32).astype(BF)
    queries = queries.reshape(length, heads, DN + DR)
    plain_latent = kv_latent[:, :KL]
    keys = (
        jnp.dot(plain_latent, key_up, preferred_element_type=F32)
        .astype(BF)
        .reshape(length, heads, DN)
    )
    values = (
        jnp.dot(plain_latent, value_up, preferred_element_type=F32)
        .astype(BF)
        .reshape(length, heads, DN)
    )
    key_rot = jnp.broadcast_to(kv_latent[:, None, KL:], (length, heads, DR))
    attn, pull = jax.vjp(attend, queries[..., :DN], queries[..., DN:], keys, key_rot, values)
    grad_plain, grad_rot, key_grad, rot_grad, value_grad = pull(
        out_grad.reshape(length, heads, DN).astype(F32)
    )
    q_grad = jnp.concatenate([grad_plain, grad_rot], axis=-1).reshape(length, heads * (DN + DR))
    key_grad = key_grad.reshape(length, heads * DN)
    value_grad = value_grad.reshape(length, heads * DN)
    rot_sum = jnp.sum(rot_grad.astype(F32), axis=1)
    term_q = transposed(q_grad, query_up)
    term_kv = transposed(key_grad, key_up) + transposed(value_grad, value_up)
    lat = jnp.concatenate(
        [term_q, term_kv, rot_sum, jnp.zeros((length, LAT - QL - KL - DR), F32)], axis=1
    )
    grad_wq = jnp.dot(query_latent.T, q_grad, preferred_element_type=F32)
    grad_wkv = jnp.dot(
        plain_latent.T, jnp.concatenate([key_grad, value_grad], axis=1), preferred_element_type=F32
    )
    width = lax.axis_size("head")
    count = (QL * query_up.shape[1] + 2 * KL * key_up.shape[1]) * width
    gq, gkv, s, lat8 = communicate(grad_wq, grad_wkv, lat)
    return tuple(finish(count, s, lat8, gq, gkv))


def solution(mesh):
    placed = (
        P("dp", None),
        P("dp", None),
        P("dp", "head"),
        P(None, "head"),
        P(None, "head"),
        P(None, "head"),
    )
    return jax.shard_map(
        per_device,
        mesh=mesh,
        in_specs=placed,
        out_specs=(
            P(("dp", "head"), None),
            P(("dp", "head"), None),
            P(None, "head"),
            P(None, "head"),
            P(None, "head"),
        ),
        check_vma=False,
    )
```

```python
import functools

import jax
import jax.numpy as jnp
import numpy as np
from jax import lax
from jax.experimental import pallas as pl
from jax.experimental.pallas import tpu as pltpu
from jax.sharding import PartitionSpec as P

QL = 1536
KL = 512
DN = 128
DR = 64
DQ = DN + DR
ROWS = 256
HEADS = 4
LAT = 2176

max_rms = 1.0
eps = 1e-06

MESH = pl.DeviceIdType.MESH
BF = jnp.bfloat16
F32 = jnp.float32

PIECES = (
    ("v", 0, 0, 512, 512, "XAB"),
    ("q", 0, 0, 768, 384, "ABX"),
    ("q", 768, 0, 768, 384, "BXA"),
    ("k", 0, 0, 512, 512, "XAB"),
    ("q", 0, 384, 768, 384, "ABX"),
    ("q", 768, 384, 768, 384, "BXA"),
)
N = len(PIECES)
CHUNK = 32


def tables():
    half = DR // 2
    freqs = np.float32(10000.0) ** (np.float32(-2.0) * np.arange(half, dtype=np.float32) / DR)
    angle = np.arange(ROWS, dtype=np.float32)[:, None] * freqs.astype(np.float32)[None, :]
    cosine, sine = np.cos(angle), np.sin(angle)
    swap = np.zeros((DR, DR), np.float32)
    for i in range(half):
        swap[half + i, i] = -1.0
        swap[i, half + i] = 1.0
    trig = np.stack([np.concatenate([t, t], axis=1) for t in (cosine, sine)])
    return trig.astype(np.float32), swap


def for_rows(rows, step, body):
    def one(i, carry):
        body(pl.multiple_of(i * step, step))
        return carry

    lax.fori_loop(0, rows // step, one, 0)


def places():
    d, h = lax.axis_index("dp"), lax.axis_index("head")
    y, xh = d // 2, d % 2
    b, y0 = y // 2, y % 2
    a = (y0 + b) % 2
    z, r = h // 4, h % 4
    xl, c = r // 2, r % 2
    bits = {"A": a, "B": b, "X": xh}
    peer = {
        "A": (2 * (y + 1 - 2 * y0) + xh, h),
        "B": (2 * (3 - y) + xh, h),
        "X": (2 * y + 1 - xh, h),
        "C": (d, h + 1 - 2 * c),
        "L": (d, h + 2 - 4 * xl),
    }
    for k in range(1, 8):
        peer["Z%d" % k] = (d, (h + 4 * k) % 32)
    return bits, peer, z, xl, c


def dot(left, right):
    return jnp.dot(left, right, preferred_element_type=F32)


def dot_nt(left, right):
    return lax.dot_general(left, right, (((1,), (1,)), ((), ())), preferred_element_type=F32)


def dot_tn(left, right):
    return lax.dot_general(left, right, (((0,), (0,)), ((), ())), preferred_element_type=F32)


def step_kernel(
    ql_hbm, kvl_hbm, dy_hbm, wq_hbm, wk_hbm, wv_hbm, trig_hbm, swap_hbm,
    g0, g1, g2, g3, g4, g5, s_out, lat_out,
    ql, kvlt, dy, wq, wk, wv, trig, swap,
    qlt, dqs, dks, dvs,
    stg0, stg1, stg2, stg3, stg4, stg5,
    rcv0, rcv1, rcv2, rcv3, rcv4, rcv5,
    ra0, ra1, ra2, ra3, ra4, ra5,
    rb0, rb1, rb2, rb3, rb4, rb5,
    lat, lrecv, lsum, zs, zr, lx, lxr,
    sv, sr, sz,
    in_sem, rs_send, rs_recv, ag_send, ag_recv, l_send, l_recv, s_send, s_recv,
):
    loads = [
        pltpu.make_async_copy(src, dst, in_sem.at[i])
        for i, (src, dst) in enumerate((
            (kvl_hbm, kvlt), (wk_hbm, wk), (wv_hbm, wv), (ql_hbm, ql), (wq_hbm, wq),
            (dy_hbm, dy), (trig_hbm, trig), (swap_hbm, swap),
        ))
    ]
    for load in loads:
        load.start()
    bits, peer, z, xl, c = places()
    barrier = pltpu.get_barrier_semaphore()
    for where in peer.values():
        pl.semaphore_signal(barrier, inc=1, device_id=where, device_id_type=MESH)

    g = (g0, g1, g2, g3, g4, g5)
    stg = (stg0, stg1, stg2, stg3, stg4, stg5)
    rcv = (rcv0, rcv1, rcv2, rcv3, rcv4, rcv5)
    red = ((ra0, rb0), (ra1, rb1), (ra2, rb2), (ra3, rb3), (ra4, rb4), (ra5, rb5))

    for load in loads[:3]:
        load.wait()
    plain = jnp.transpose(kvlt[:KL, :])
    key_rot = jnp.transpose(kvlt[KL:, :])
    keys = dot(plain, wk[...]).astype(BF)
    values = dot(plain, wv[...]).astype(BF)
    for load in loads[3:]:
        load.wait()
    queries = dot(ql[...], wq[...]).astype(BF)
    qlt[...] = jnp.transpose(ql[...])

    scale = 1.0 / DQ**0.5
    allowed = lax.broadcasted_iota(jnp.int32, (ROWS, ROWS), 0) <= lax.broadcasted_iota(
        jnp.int32, (ROWS, ROWS), 1
    )
    cosine, sine = trig[0], trig[1]
    turn = swap[...]
    rot = jnp.zeros((ROWS, DR), F32)
    parts = []
    for n in range(HEADS):
        q_plain = queries[:, DQ * n : DQ * n + DN]
        q_rot = queries[:, DQ * n + DN : DQ * (n + 1)]
        q_rope = (q_rot.astype(F32) * cosine + dot(q_rot, turn) * sine).astype(BF)
        key = keys[:, DN * n : DN * (n + 1)]
        value = values[:, DN * n : DN * (n + 1)]
        grad = dy[:, DN * n : DN * (n + 1)]
        q_all = jnp.concatenate([q_plain, q_rope], axis=1)
        k_all = jnp.concatenate([key, key_rot], axis=1)
        scores = jnp.where(allowed, dot_nt(k_all, q_all) * scale, -jnp.inf)
        top = jnp.max(scores, axis=0, keepdims=True)
        weights = jnp.exp(scores - top)
        probs = weights / jnp.sum(weights, axis=0, keepdims=True)
        dvs[:, DN * n : DN * (n + 1)] = dot(probs.astype(BF), grad).astype(BF)
        dp = dot_nt(value, grad)
        mean = jnp.sum(dp * probs, axis=0, keepdims=True)
        ds = (probs * (dp - mean) * scale).astype(BF)
        dk = dot(ds, q_all)
        dks[:, DN * n : DN * (n + 1)] = dk[:, :DN].astype(BF)
        rot = rot + dk[:, DN:].astype(BF).astype(F32)
        dq = dot_tn(ds, k_all)
        d_rope = dq[:, DN:].astype(BF)
        d_rot = d_rope.astype(F32) * cosine + dot_nt(d_rope, turn) * sine
        parts.append(jnp.concatenate([dq[:, :DN].astype(BF), d_rot.astype(BF)], axis=1))
        if n % 2:
            dqs[:, DQ * (n - 1) : DQ * (n + 1)] = jnp.concatenate(parts, axis=1)
            parts = []

    def remote(src, dst, send, recv, where):
        copy = pltpu.make_async_remote_copy(
            src_ref=src, dst_ref=dst, send_sem=send, recv_sem=recv,
            device_id=peer[where], device_id_type=MESH,
        )
        copy.start()
        return copy

    def product(p, lo, n):
        which, r0, c0, _, cols, _ = PIECES[p]
        if which == "q":
            return dot(qlt[pl.ds(r0 + lo, n), :], dqs[:, c0 : c0 + cols])
        return dot(kvlt[pl.ds(lo, n), :], (dks if which == "k" else dvs)[...])

    def area(p, s):
        rows = PIECES[p][3]
        return (0, rows // 2, rows // 2 + rows // 4)[s], rows >> (s + 1)

    def rs_send_off(p, s):
        off, n = area(p, s)
        return remote(
            stg[p].at[pl.ds(off, n)], rcv[p].at[pl.ds(off, n)],
            rs_send.at[p, s], rs_recv.at[p, s], PIECES[p][5][s],
        )

    def rs_first(p):
        off, n = area(p, 0)
        away = pl.multiple_of((1 - bits[PIECES[p][5][0]]) * n, 128)
        for i in range(0, n, 128):
            stg[p][i : i + 128, :] = product(p, away + i, 128).astype(BF)
        return rs_send_off(p, 0)

    def rs_keep(p):
        off, n = area(p, 0)
        keep = pl.multiple_of(bits[PIECES[p][5][0]] * n, 128)
        for i in range(0, n, 128):
            red[p][0][i : i + 128, :] = product(p, keep + i, 128)

    def rs_second(p, copy):
        copy.wait()
        off, n = area(p, 1)
        bit = bits[PIECES[p][5][1]]
        away, keep = (1 - bit) * n, bit * n

        def total(lo):
            return red[p][0][pl.ds(lo, CHUNK), :] + rcv[p][pl.ds(lo, CHUNK), :].astype(F32)

        def out(i):
            stg[p][pl.ds(off + i, CHUNK), :] = total(pl.multiple_of(away + i, CHUNK)).astype(BF)

        for_rows(n, CHUNK, out)
        sent = rs_send_off(p, 1)

        def hold(i):
            red[p][1][pl.ds(i, CHUNK), :] = total(pl.multiple_of(keep + i, CHUNK))

        for_rows(n, CHUNK, hold)
        return sent

    def rs_third(p, copy):
        copy.wait()
        before, _ = area(p, 1)
        off, n = area(p, 2)
        bit = bits[PIECES[p][5][2]]
        away = (1 - bit) * n

        def out(i):
            lo = pl.multiple_of(away + i, CHUNK)
            stg[p][pl.ds(off + i, CHUNK), :] = (
                red[p][1][pl.ds(lo, CHUNK), :]
                + rcv[p][pl.ds(pl.multiple_of(before + lo, CHUNK), CHUNK), :].astype(F32)
            ).astype(BF)

        for_rows(n, CHUNK, out)
        return rs_send_off(p, 2)

    def owned(p, s):
        rows, order = PIECES[p][3], PIECES[p][5]
        lo = 0
        for t in range(s + 1):
            lo = lo + bits[order[t]] * (rows >> (t + 1))
        return pl.multiple_of(lo, CHUNK)

    def rs_last(p, copy):
        copy.wait()
        before, _ = area(p, 1)
        off, n = area(p, 2)
        keep = bits[PIECES[p][5][2]] * n
        lo = owned(p, 2)

        def body(i):
            at = pl.multiple_of(keep + i, CHUNK)
            total = (
                red[p][1][pl.ds(at, CHUNK), :]
                + rcv[p][pl.ds(pl.multiple_of(before + at, CHUNK), CHUNK), :].astype(F32)
                + rcv[p][pl.ds(off + i, CHUNK), :].astype(F32)
            )
            g[p][pl.ds(pl.multiple_of(lo + i, CHUNK), CHUNK), :] = total.astype(BF)
            square = total * total
            part = square[:, :128]
            for j in range(1, PIECES[p][4] // 128):
                part = part + square[:, 128 * j : 128 * (j + 1)]
            sv[0] = sv[0] + part[:8] + part[8:16] + part[16:24] + part[24:32]

        for_rows(n, CHUNK, body)

    def ag_start(p, s):
        block = g[p].at[pl.ds(owned(p, s), PIECES[p][3] >> (s + 1))]
        return remote(block, block, ag_send.at[p, s], ag_recv.at[p, s], PIECES[p][5][s])

    pl.semaphore_wait(barrier, len(peer))
    first = [rs_first(p) for p in range(N)]
    for p in range(N):
        rs_keep(p)

    lat[:, :, :, :QL] = dot_nt(dqs[...], wq[...]).reshape(16, 2, 8, QL)
    lat[:, :, :, QL : QL + KL] = (dot_nt(dks[...], wk[...]) + dot_nt(dvs[...], wv[...])).reshape(
        16, 2, 8, KL
    )
    lat[:, :, :, QL + KL :] = jnp.concatenate([rot, jnp.zeros((ROWS, DR), F32)], axis=1).reshape(
        16, 2, 8, 128
    )
    core = remote(lat.at[:, 1 - c], lrecv, l_send.at[0], l_recv.at[0], "C")
    second = [None] * N
    for p in range(3):
        second[p] = rs_second(p, first[p])
    core.wait()

    def core_body(k, carry):
        lsum[k] = lat[k, c] + lrecv[k]
        return carry

    lax.fori_loop(0, 16, core_body, 0)

    def zs_body(k, carry):
        zs[k] = jnp.concatenate([lsum[2 * k], lsum[2 * k + 1]], axis=0).astype(BF)
        return carry

    lax.fori_loop(0, 8, zs_body, 0)
    zcopies = [
        remote(zs.at[(z + k) % 8], zr.at[k - 1], l_send.at[k], l_recv.at[k], "Z%d" % k)
        for k in range(1, 8)
    ]
    for p in range(3, N):
        second[p] = rs_second(p, first[p])
    third = [rs_third(p, second[p]) for p in range(N)]
    sv[0] = jnp.zeros((8, 128), F32)
    gather = []
    for p in range(N):
        rs_last(p, third[p])
        gather.append(ag_start(p, 2))

    def s_step(i, dim):
        return remote(sv.at[i], sr.at[i], s_send.at[i], s_recv.at[i], dim)

    def s_add(copy, i):
        copy.wait()
        sv[i + 1] = sv[i] + sr[i]

    s0 = s_step(0, "A")
    s_add(s0, 0)
    s1 = s_step(1, "C")
    s_add(s1, 1)
    s2 = s_step(2, "B")
    later = []
    for p in range(N):
        gather[p].wait()
        later.append(ag_start(p, 1))
    s_add(s2, 2)
    s3 = s_step(3, "L")
    for copy in zcopies:
        copy.wait()
    lx[0] = lsum[2 * z]
    lx[1] = lsum[2 * z + 1]
    for k in range(7):
        got = zr[k].astype(F32)
        lx[0] = lx[0] + got[:8]
        lx[1] = lx[1] + got[8:]
    xcopy = remote(lx.at[1 - xl], lxr, l_send.at[8], l_recv.at[8], "L")
    s_add(s3, 3)
    s4 = s_step(4, "X")
    last = []
    for p in range(N):
        later[p].wait()
        last.append(ag_start(p, 0))
    s_add(s4, 4)
    szc = [
        remote(sv.at[5], sz.at[z], s_send.at[4 + k], s_recv.at[4 + k], "Z%d" % k)
        for k in range(1, 8)
    ]
    sz[z] = sv[5]
    xcopy.wait()
    lat_out[...] = lx[xl] + lxr[...]
    for copy in szc:
        copy.wait()
    s_out[...] = sz[...]
    for copy in last:
        copy.wait()


def step(ql, kvl, dy, wq, wk, wv):
    trig, swap = tables()
    vmem = pl.BlockSpec(memory_space=pltpu.VMEM)
    hbm = pl.BlockSpec(memory_space=pltpu.HBM)

    def moved(p):
        rows = PIECES[p][3]
        return rows // 2 + rows // 4 + rows // 8

    scratch = [
        pltpu.VMEM((ROWS, QL), BF),
        pltpu.VMEM((KL + DR, ROWS), BF),
        pltpu.VMEM((ROWS, HEADS * DN), BF),
        pltpu.VMEM((QL, HEADS * DQ), BF),
        pltpu.VMEM((KL, HEADS * DN), BF),
        pltpu.VMEM((KL, HEADS * DN), BF),
        pltpu.VMEM((2, ROWS, DR), F32),
        pltpu.VMEM((DR, DR), BF),
        pltpu.VMEM((QL, ROWS), BF),
        pltpu.VMEM((ROWS, HEADS * DQ), BF),
        pltpu.VMEM((ROWS, HEADS * DN), BF),
        pltpu.VMEM((ROWS, HEADS * DN), BF),
    ]
    scratch += [pltpu.VMEM((moved(p), PIECES[p][4]), BF) for p in range(N)] * 2
    scratch += [pltpu.VMEM((PIECES[p][3] // 2, PIECES[p][4]), F32) for p in range(N)]
    scratch += [pltpu.VMEM((PIECES[p][3] // 4, PIECES[p][4]), F32) for p in range(N)]
    scratch += [
        pltpu.VMEM((16, 2, 8, LAT), F32),
        pltpu.VMEM((16, 8, LAT), F32),
        pltpu.VMEM((16, 8, LAT), F32),
        pltpu.VMEM((8, 16, LAT), BF),
        pltpu.VMEM((7, 16, LAT), BF),
        pltpu.VMEM((2, 8, LAT), F32),
        pltpu.VMEM((8, LAT), F32),
        pltpu.VMEM((6, 8, 128), F32),
        pltpu.VMEM((5, 8, 128), F32),
        pltpu.VMEM((8, 8, 128), F32),
    ]
    dma = pltpu.SemaphoreType.DMA
    scratch += [dma((8,)), dma((N, 3)), dma((N, 3)), dma((N, 3)), dma((N, 3))]
    scratch += [dma((9,)), dma((9,)), dma((12,)), dma((12,))]
    return pl.pallas_call(
        step_kernel,
        out_shape=tuple(jax.ShapeDtypeStruct((p[3], p[4]), BF) for p in PIECES)
        + (jax.ShapeDtypeStruct((8, 8, 128), F32), jax.ShapeDtypeStruct((8, LAT), F32)),
        in_specs=[hbm] * 8,
        out_specs=(vmem,) * (N + 2),
        scratch_shapes=scratch,
        name="step",
        compiler_params=pltpu.CompilerParams(
            collective_id=0, has_side_effects=True, vmem_limit_bytes=46 << 20
        ),
    )(*(pltpu.with_memory_space_constraint(t, pltpu.HBM) for t in (ql, kvl, dy, wq, wk, wv, jnp.asarray(trig), jnp.asarray(swap, BF))))


def finish_kernel(
    count, s_ref, lat_ref, g0, g1, g2, g3, g4, g5,
    ql_out, kvl_out, q_out, k_out, v_out,
    b0, b1, b2, b3, b4, b5, kvl, sem,
):
    kvl[...] = lat_ref[:, QL : QL + KL + DR]
    copies = [
        pltpu.make_async_copy(lat_ref.at[:, pl.ds(0, QL)], ql_out, sem.at[N]),
        pltpu.make_async_copy(kvl, kvl_out, sem.at[N + 1]),
    ]
    for copy in copies:
        copy.start()
    total = jnp.sum(s_ref[...], axis=0)
    total = jnp.sum(total, axis=0, keepdims=True)
    total = jnp.sum(total, axis=1, keepdims=True)
    factor = jnp.minimum(1.0, max_rms * count**0.5 / jnp.sqrt(total + eps))
    for p, (src, buf) in enumerate(zip((g0, g1, g2, g3, g4, g5), (b0, b1, b2, b3, b4, b5))):
        which, r0, c0, rows, cols, _ = PIECES[p]

        def body(i):
            buf[pl.ds(i, CHUNK), :] = (src[pl.ds(i, CHUNK), :].astype(F32) * factor).astype(BF)

        for_rows(rows, CHUNK, body)
        if which == "q":
            dst = q_out.at[pl.ds(r0, rows), pl.ds(c0, cols)]
        else:
            dst = k_out if which == "k" else v_out
        copy = pltpu.make_async_copy(buf, dst, sem.at[p])
        copy.start()
        copies.append(copy)
    for copy in copies:
        copy.wait()


def finish(count, s, lat, pieces):
    vmem = pl.BlockSpec(memory_space=pltpu.VMEM)
    hbm = pl.BlockSpec(memory_space=pl.ANY)
    return pl.pallas_call(
        functools.partial(finish_kernel, count),
        out_shape=(
            jax.ShapeDtypeStruct((8, QL), F32),
            jax.ShapeDtypeStruct((8, KL + DR), F32),
            jax.ShapeDtypeStruct((QL, HEADS * DQ), BF),
            jax.ShapeDtypeStruct((KL, HEADS * DN), BF),
            jax.ShapeDtypeStruct((KL, HEADS * DN), BF),
        ),
        in_specs=[vmem] * (N + 2),
        out_specs=(hbm,) * 5,
        scratch_shapes=[pltpu.VMEM((p[3], p[4]), BF) for p in PIECES]
        + [pltpu.VMEM((8, KL + DR), F32), pltpu.SemaphoreType.DMA((N + 2,))],
        name="finish",
        compiler_params=pltpu.CompilerParams(vmem_limit_bytes=16 << 20),
    )(s, lat, *pieces)


def per_device(query_latent, kv_latent, out_grad, query_up, key_up, value_up):
    width = lax.axis_size("head")
    count = (QL * query_up.shape[1] + 2 * KL * key_up.shape[1]) * width
    *pieces, s, lat = step(query_latent, kv_latent.T, out_grad, query_up, key_up, value_up)
    return tuple(finish(count, s, lat, pieces))


def solution(mesh):
    placed = (
        P("dp", None),
        P("dp", None),
        P("dp", "head"),
        P(None, "head"),
        P(None, "head"),
        P(None, "head"),
    )
    return jax.shard_map(
        per_device,
        mesh=mesh,
        in_specs=placed,
        out_specs=(
            P(("dp", "head"), None),
            P(("dp", "head"), None),
            P(None, "head"),
            P(None, "head"),
            P(None, "head"),
        ),
        check_vma=False,
    )
```

```python
import functools

import jax
import jax.numpy as jnp
import numpy as np
from jax import lax
from jax.experimental import pallas as pl
from jax.experimental.pallas import tpu as pltpu
from jax.sharding import PartitionSpec as P

QL = 1536
KL = 512
DN = 128
DR = 64
DQ = DN + DR
ROWS = 256
HEADS = 4
LAT = 2176

max_rms = 1.0
eps = 1e-06

MESH = pl.DeviceIdType.MESH
BF = jnp.bfloat16
F32 = jnp.float32

PAIRS = 2
QC = 2 * DQ
KC = 4 * DN
SHAPES = ((768, QC), (768, QC), (512, KC))
G = PAIRS * len(SHAPES)
ORDERS = ("ABX", "BXA", "XAB")
SUB = 2
PIECES = tuple(
    (3 * j + kind, kind, SHAPES[kind][0] // SUB * u, SHAPES[kind][0] // SUB)
    for j in range(PAIRS)
    for u in range(SUB)
    for kind in range(3)
)
N = len(PIECES)
STEPS = (48, 48, 32)


def tables():
    half = DR // 2
    freqs = np.float32(10000.0) ** (np.float32(-2.0) * np.arange(half, dtype=np.float32) / DR)
    angle = np.arange(ROWS, dtype=np.float32)[:, None] * freqs.astype(np.float32)[None, :]
    cosine, sine = np.cos(angle), np.sin(angle)
    swap = np.zeros((DR, DR), np.float32)
    for i in range(half):
        swap[half + i, i] = -1.0
        swap[i, half + i] = 1.0
    trig = np.stack([np.concatenate([t, t], axis=1) for t in (cosine, sine)])
    return trig.astype(np.float32), swap


def for_rows(rows, step, body):
    def one(i, carry):
        body(pl.multiple_of(i * step, step))
        return carry

    lax.fori_loop(0, rows // step, one, 0)


def places():
    d, h = lax.axis_index("dp"), lax.axis_index("head")
    y, xh = d // 2, d % 2
    b, y0 = y // 2, y % 2
    a = (y0 + b) % 2
    z, r = h // 4, h % 4
    xl, c = r // 2, r % 2
    bits = {"A": a, "B": b, "X": xh}
    ya, yb, yab = y + 1 - 2 * y0, 3 - y, 2 - y + 2 * y0
    peer = {
        "A": (2 * ya + xh, h),
        "B": (2 * yb + xh, h),
        "X": (2 * y + 1 - xh, h),
        "AB": (2 * yab + xh, h),
        "AX": (2 * ya + 1 - xh, h),
        "BX": (2 * yb + 1 - xh, h),
        "ABX": (2 * yab + 1 - xh, h),
        "C": (d, h + 1 - 2 * c),
        "L": (d, h + 2 - 4 * xl),
    }
    for k in range(1, 8):
        peer["Z%d" % k] = (d, (h + 4 * k) % 32)
    return bits, peer, d, z, xl, c


def dot(left, right):
    return jnp.dot(left, right, preferred_element_type=F32)


def dot_nt(left, right):
    return lax.dot_general(left, right, (((1,), (1,)), ((), ())), preferred_element_type=F32)


def dot_tn(left, right):
    return lax.dot_general(left, right, (((0,), (0,)), ((), ())), preferred_element_type=F32)


def step_kernel(*refs):
    refs = list(refs)

    def take(n):
        out = refs[:n]
        del refs[:n]
        return out

    ql_hbm, kvl_hbm, dy_hbm, wq_hbm, wk_hbm, wv_hbm, trig_hbm, swap_hbm = take(8)
    g = take(G)
    s_out, lat_out = take(2)
    ql, kvlt, dy, wq, wk, wv, trig, swap, qlt, dqs, dkv = take(11)
    stg, rcv, ra, rb = take(N), take(N), take(N), take(N)
    lat, lrecv, lsum, zs, zr, lx, lxr, sq, sd, sl, slr, sc, scr, sf, sz = take(15)
    in_sem, rs_send, rs_recv, ag_send, ag_recv, l_send, l_recv, s_send, s_recv = take(9)

    loads = [
        pltpu.make_async_copy(src, dst, in_sem.at[i])
        for i, (src, dst) in enumerate((
            (kvl_hbm, kvlt), (wk_hbm, wk), (wv_hbm, wv), (ql_hbm, ql),
            (wq_hbm.at[:, pl.ds(0, QC)], wq.at[0]), (dy_hbm, dy), (trig_hbm, trig), (swap_hbm, swap),
            (wq_hbm.at[:, pl.ds(QC, QC)], wq.at[1]),
        ))
    ]
    for load in loads:
        load.start()
    bits, peer, d, z, xl, c = places()
    barrier = pltpu.get_barrier_semaphore()
    for where in peer.values():
        pl.semaphore_signal(barrier, inc=1, device_id=where, device_id_type=MESH)

    def remote(src, dst, send, recv, where):
        copy = pltpu.make_async_remote_copy(
            src_ref=src, dst_ref=dst, send_sem=send, recv_sem=recv,
            device_id=peer[where], device_id_type=MESH,
        )
        copy.start()
        return copy

    def cut(p):
        return PIECES[p][1], PIECES[p][3], STEPS[PIECES[p][1]]

    def product(p, lo, n):
        array, kind, r0, _ = PIECES[p]
        if kind == 2:
            return dot(kvlt[pl.ds(r0 + lo, n), :], dkv[array // 3])
        return dot(qlt[pl.ds(768 * kind + r0 + lo, n), :], dqs[array // 3])

    def area(p, s):
        rows = cut(p)[1]
        return (0, rows // 2, rows // 2 + rows // 4)[s], rows >> (s + 1)

    def dim(p, s):
        return ORDERS[cut(p)[0]][s]

    def rs_send_off(p, s):
        off, n = area(p, s)
        return remote(
            stg[p].at[pl.ds(off, n)], rcv[p].at[pl.ds(off, n)],
            rs_send.at[p, s], rs_recv.at[p, s], dim(p, s),
        )

    def rs_first(p):
        off, n = area(p, 0)
        away = pl.multiple_of((1 - bits[dim(p, 0)]) * n, 64)
        stg[p][:n, :] = product(p, away, n).astype(BF)
        return rs_send_off(p, 0)

    def rs_keep(p):
        off, n = area(p, 0)
        keep = pl.multiple_of(bits[dim(p, 0)] * n, 64)
        ra[p][...] = product(p, keep, n)

    def rs_second(p, copy):
        copy.wait()
        off, n = area(p, 1)
        bit = bits[dim(p, 1)]
        away, keep = (1 - bit) * n, bit * n
        rows = cut(p)[2]

        def total(lo):
            return ra[p][pl.ds(lo, rows), :] + rcv[p][pl.ds(lo, rows), :].astype(F32)

        def out(i):
            stg[p][pl.ds(off + i, rows), :] = total(pl.multiple_of(away + i, 16)).astype(BF)

        for_rows(n, rows, out)
        sent = rs_send_off(p, 1)

        def hold(i):
            rb[p][pl.ds(i, rows), :] = total(pl.multiple_of(keep + i, 16))

        for_rows(n, rows, hold)
        return sent

    def rs_third(p, copy):
        copy.wait()
        before, _ = area(p, 1)
        off, n = area(p, 2)
        away = (1 - bits[dim(p, 2)]) * n
        rows = cut(p)[2]

        def out(i):
            lo = pl.multiple_of(away + i, 16)
            stg[p][pl.ds(off + i, rows), :] = (
                rb[p][pl.ds(lo, rows), :]
                + rcv[p][pl.ds(pl.multiple_of(before + lo, 16), rows), :].astype(F32)
            ).astype(BF)

        for_rows(n, rows, out)
        return rs_send_off(p, 2)

    def owned(p, s):
        lo = PIECES[p][2]
        for t in range(s + 1):
            lo = lo + bits[dim(p, t)] * (cut(p)[1] >> (t + 1))
        return pl.multiple_of(lo, 16)

    def rs_last(p, copy):
        copy.wait()
        before, _ = area(p, 1)
        off, n = area(p, 2)
        keep = bits[dim(p, 2)] * n
        lo = owned(p, 2)
        rows = cut(p)[2]
        out = g[PIECES[p][0]]

        def body(i):
            at = pl.multiple_of(keep + i, 16)
            total = (
                rb[p][pl.ds(at, rows), :]
                + rcv[p][pl.ds(pl.multiple_of(before + at, 16), rows), :].astype(F32)
                + rcv[p][pl.ds(off + i, rows), :].astype(F32)
            )
            out[pl.ds(pl.multiple_of(lo + i, 16), rows), :] = total.astype(BF)
            square = total * total
            part = square[:, :128]
            for j in range(1, square.shape[1] // 128):
                part = part + square[:, 128 * j : 128 * (j + 1)]
            left = sq[...]
            for j in range(0, rows, 8):
                left = left + part[j : j + 8]
            sq[...] = left

        for_rows(n, rows, body)

    def ag_start(p, s):
        block = g[PIECES[p][0]].at[pl.ds(owned(p, s), cut(p)[1] >> (s + 1))]
        return remote(block, block, ag_send.at[p, s], ag_recv.at[p, s], dim(p, s))

    for load in loads[:3]:
        load.wait()
    plain = jnp.transpose(kvlt[:KL, :])
    key_rot = jnp.transpose(kvlt[KL:, :])
    scale = 1.0 / DQ**0.5
    allowed = lax.broadcasted_iota(jnp.int32, (ROWS, ROWS), 0) <= lax.broadcasted_iota(
        jnp.int32, (ROWS, ROWS), 1
    )
    rot = jnp.zeros((ROWS, DR), F32)
    moving = []
    for j in range(PAIRS):
        cols = slice(2 * DN * j, 2 * DN * (j + 1))
        keys = dot(plain, wk[:, cols]).astype(BF)
        values = dot(plain, wv[:, cols]).astype(BF)
        if j == 0:
            for load in loads[3:8]:
                load.wait()
            cosine, sine = trig[0], trig[1]
            turn = swap[...]
        else:
            loads[8].wait()
        queries = dot(ql[...], wq[j]).astype(BF)
        if j == 0:
            qlt[...] = jnp.transpose(ql[...])
        parts = []
        for n in range(2):
            q_plain = queries[:, DQ * n : DQ * n + DN]
            q_rot = queries[:, DQ * n + DN : DQ * (n + 1)]
            q_rope = (q_rot.astype(F32) * cosine + dot(q_rot, turn) * sine).astype(BF)
            key = keys[:, DN * n : DN * (n + 1)]
            value = values[:, DN * n : DN * (n + 1)]
            grad = dy[:, 2 * DN * j + DN * n : 2 * DN * j + DN * (n + 1)]
            q_all = jnp.concatenate([q_plain, q_rope], axis=1)
            k_all = jnp.concatenate([key, key_rot], axis=1)
            scores = jnp.where(allowed, dot_nt(k_all, q_all) * scale, -jnp.inf)
            top = jnp.max(scores, axis=0, keepdims=True)
            weights = jnp.exp(scores - top)
            probs = weights / jnp.sum(weights, axis=0, keepdims=True)
            dkv[j, :, 2 * DN + DN * n : 2 * DN + DN * (n + 1)] = dot(
                probs.astype(BF), grad
            ).astype(BF)
            dp = dot_nt(value, grad)
            mean = jnp.sum(dp * probs, axis=0, keepdims=True)
            ds = (probs * (dp - mean) * scale).astype(BF)
            dk = dot(ds, q_all)
            dkv[j, :, DN * n : DN * (n + 1)] = dk[:, :DN].astype(BF)
            rot = rot + dk[:, DN:].astype(BF).astype(F32)
            dq = dot_tn(ds, k_all)
            d_rope = dq[:, DN:].astype(BF)
            d_rot = d_rope.astype(F32) * cosine + dot_nt(d_rope, turn) * sine
            parts.append(jnp.concatenate([dq[:, :DN].astype(BF), d_rot.astype(BF)], axis=1))
        dqs[j] = jnp.concatenate(parts, axis=1)
        if j == 0:
            pl.semaphore_wait(barrier, len(peer))
        for p in range(N // PAIRS):
            moving.append(rs_first(N // PAIRS * j + p))

    lat[:, :, :, :QL] = (dot_nt(dqs[0], wq[0]) + dot_nt(dqs[1], wq[1])).reshape(16, 2, 8, QL)
    term = dot_nt(dkv[0, :, : 2 * DN], wk[:, : 2 * DN]) + dot_nt(dkv[1, :, : 2 * DN], wk[:, 2 * DN :])
    term = term + dot_nt(dkv[0, :, 2 * DN :], wv[:, : 2 * DN])
    term = term + dot_nt(dkv[1, :, 2 * DN :], wv[:, 2 * DN :])
    lat[:, :, :, QL : QL + KL] = term.reshape(16, 2, 8, KL)
    lat[:, :, :, QL + KL :] = jnp.concatenate([rot, jnp.zeros((ROWS, DR), F32)], axis=1).reshape(
        16, 2, 8, 128
    )
    core = remote(lat.at[:, 1 - c], lrecv, l_send.at[0], l_recv.at[0], "C")
    turns = [p + q for p in range(0, N, 3) for q in (0, 1, 2)]
    for p in turns:
        rs_keep(p)
    for p in turns[:3]:
        moving[p] = rs_second(p, moving[p])
    core.wait()

    def core_body(k, carry):
        lsum[k] = lat[k, c] + lrecv[k]
        return carry

    lax.fori_loop(0, 16, core_body, 0)

    def zs_body(k, carry):
        zs[k] = jnp.concatenate([lsum[2 * k], lsum[2 * k + 1]], axis=0).astype(BF)
        return carry

    lax.fori_loop(0, 8, zs_body, 0)
    zcopies = [
        remote(zs.at[(z + k) % 8], zr.at[k - 1], l_send.at[k], l_recv.at[k], "Z%d" % k)
        for k in range(1, 8)
    ]
    for p in turns[3:]:
        moving[p] = rs_second(p, moving[p])
    for p in turns:
        moving[p] = rs_third(p, moving[p])
    sq[...] = jnp.zeros((8, 128), F32)
    for p in turns:
        rs_last(p, moving[p])
        moving[p] = ag_start(p, 2)

    cube = [
        remote(sq, sd.at[d], s_send.at[i], s_recv.at[i], where)
        for i, where in enumerate(("A", "B", "X", "AB", "AX", "BX", "ABX"))
    ]
    sd[d] = sq[...]
    for copy in zcopies:
        copy.wait()
    lx[0] = lsum[2 * z]
    lx[1] = lsum[2 * z + 1]
    for k in range(7):
        got = zr[k].astype(F32)
        lx[0] = lx[0] + got[:8]
        lx[1] = lx[1] + got[8:]
    xcopy = remote(lx.at[1 - xl], lxr, l_send.at[8], l_recv.at[8], "L")
    for p in turns:
        moving[p].wait()
        moving[p] = ag_start(p, 1)
    for copy in cube:
        copy.wait()
    total = sd[0]
    for i in range(1, 8):
        total = total + sd[i]
    sl[...] = total
    ls = remote(sl, slr, s_send.at[7], s_recv.at[7], "L")
    for p in turns:
        moving[p].wait()
        moving[p] = ag_start(p, 0)
    ls.wait()
    sc[...] = sl[...] + slr[...]
    cs = remote(sc, scr, s_send.at[8], s_recv.at[8], "C")
    xcopy.wait()
    lat_out[...] = lx[xl] + lxr[...]
    cs.wait()
    sf[...] = sc[...] + scr[...]
    zsum = [
        remote(sf, sz.at[z], s_send.at[8 + k], s_recv.at[8 + k], "Z%d" % k) for k in range(1, 8)
    ]
    sz[z] = sf[...]
    for copy in zsum:
        copy.wait()
    s_out[...] = sz[...]
    for copy in moving:
        copy.wait()


def step(ql, kvl, dy, wq, wk, wv):
    trig, swap = tables()
    vmem = pl.BlockSpec(memory_space=pltpu.VMEM)
    hbm = pl.BlockSpec(memory_space=pltpu.HBM)

    def buffer(p, rows, dtype):
        return pltpu.VMEM((rows, SHAPES[PIECES[p][1]][1]), dtype)

    scratch = [
        pltpu.VMEM((ROWS, QL), BF),
        pltpu.VMEM((KL + DR, ROWS), BF),
        pltpu.VMEM((ROWS, HEADS * DN), BF),
        pltpu.VMEM((PAIRS, QL, QC), BF),
        pltpu.VMEM((KL, HEADS * DN), BF),
        pltpu.VMEM((KL, HEADS * DN), BF),
        pltpu.VMEM((2, ROWS, DR), F32),
        pltpu.VMEM((DR, DR), BF),
        pltpu.VMEM((QL, ROWS), BF),
        pltpu.VMEM((PAIRS, ROWS, QC), BF),
        pltpu.VMEM((PAIRS, ROWS, KC), BF),
    ]
    scratch += [buffer(p, PIECES[p][3] * 7 // 8, BF) for p in range(N)] * 2
    scratch += [buffer(p, PIECES[p][3] // 2, F32) for p in range(N)]
    scratch += [buffer(p, PIECES[p][3] // 4, F32) for p in range(N)]
    tile = (8, 128)
    scratch += [
        pltpu.VMEM((16, 2, 8, LAT), F32),
        pltpu.VMEM((16, 8, LAT), F32),
        pltpu.VMEM((16, 8, LAT), F32),
        pltpu.VMEM((8, 16, LAT), BF),
        pltpu.VMEM((7, 16, LAT), BF),
        pltpu.VMEM((2, 8, LAT), F32),
        pltpu.VMEM((8, LAT), F32),
        pltpu.VMEM(tile, F32),
        pltpu.VMEM((8,) + tile, F32),
    ]
    scratch += [pltpu.VMEM(tile, F32)] * 5 + [pltpu.VMEM((8,) + tile, F32)]
    dma = pltpu.SemaphoreType.DMA
    scratch += [dma((9,)), dma((N, 3)), dma((N, 3)), dma((N, 3)), dma((N, 3))]
    scratch += [dma((9,)), dma((9,)), dma((16,)), dma((16,))]
    args = (ql, kvl, dy, wq, wk, wv, jnp.asarray(trig), jnp.asarray(swap, BF))
    return pl.pallas_call(
        step_kernel,
        out_shape=tuple(jax.ShapeDtypeStruct(SHAPES[i % 3], BF) for i in range(G))
        + (jax.ShapeDtypeStruct((8, 8, 128), F32), jax.ShapeDtypeStruct((8, LAT), F32)),
        in_specs=[hbm] * 8,
        out_specs=(vmem,) * (G + 2),
        scratch_shapes=scratch,
        name="step",
        compiler_params=pltpu.CompilerParams(
            collective_id=0, has_side_effects=True, vmem_limit_bytes=46 << 20
        ),
    )(*(pltpu.with_memory_space_constraint(t, pltpu.HBM) for t in args))


def finish_kernel(count, *refs):
    s_ref, lat_ref = refs[:2]
    g = refs[2 : 2 + G]
    ql_out, kvl_out, q_out, k_out, v_out = refs[2 + G : 7 + G]
    buffers = refs[7 + G : 7 + 2 * G]
    kvl, sem = refs[7 + 2 * G :]
    kvl[...] = lat_ref[:, QL : QL + KL + DR]
    copies = []

    def start(src, dst):
        copy = pltpu.make_async_copy(src, dst, sem.at[len(copies)])
        copy.start()
        copies.append(copy)

    start(lat_ref.at[:, pl.ds(0, QL)], ql_out)
    start(kvl, kvl_out)
    total = jnp.sum(s_ref[...], axis=0)
    total = jnp.sum(total, axis=0, keepdims=True)
    total = jnp.sum(total, axis=1, keepdims=True)
    factor = jnp.minimum(1.0, max_rms * count**0.5 / jnp.sqrt(total + eps))
    for i in range(G):
        j, kind = i // 3, i % 3
        rows = SHAPES[kind][0] // SUB
        for u in range(SUB):
            at = pl.ds(rows * u, rows)

            def body(lo):
                where = pl.ds(pl.multiple_of(rows * u + lo, 16), 64)
                buffers[i][where, :] = (g[i][where, :].astype(F32) * factor).astype(BF)

            for_rows(rows, 64, body)
            if kind == 2:
                half = pl.ds(2 * DN * j, 2 * DN)
                start(buffers[i].at[at, pl.ds(0, 2 * DN)], k_out.at[at, half])
                start(buffers[i].at[at, pl.ds(2 * DN, 2 * DN)], v_out.at[at, half])
            else:
                start(
                    buffers[i].at[at],
                    q_out.at[pl.ds(768 * kind + rows * u, rows), pl.ds(QC * j, QC)],
                )
    for copy in copies:
        copy.wait()


def finish(count, s, lat, pieces):
    vmem = pl.BlockSpec(memory_space=pltpu.VMEM)
    hbm = pl.BlockSpec(memory_space=pl.ANY)
    return pl.pallas_call(
        functools.partial(finish_kernel, count),
        out_shape=(
            jax.ShapeDtypeStruct((8, QL), F32),
            jax.ShapeDtypeStruct((8, KL + DR), F32),
            jax.ShapeDtypeStruct((QL, HEADS * DQ), BF),
            jax.ShapeDtypeStruct((KL, HEADS * DN), BF),
            jax.ShapeDtypeStruct((KL, HEADS * DN), BF),
        ),
        in_specs=[vmem] * (G + 2),
        out_specs=(hbm,) * 5,
        scratch_shapes=[pltpu.VMEM(SHAPES[i % 3], BF) for i in range(G)]
        + [pltpu.VMEM((8, KL + DR), F32), pltpu.SemaphoreType.DMA((2 + SUB * PAIRS * 4,))],
        name="finish",
        compiler_params=pltpu.CompilerParams(vmem_limit_bytes=16 << 20),
    )(s, lat, *pieces)


def per_device(query_latent, kv_latent, out_grad, query_up, key_up, value_up):
    width = lax.axis_size("head")
    count = (QL * query_up.shape[1] + 2 * KL * key_up.shape[1]) * width
    *pieces, s, lat = step(query_latent, kv_latent.T, out_grad, query_up, key_up, value_up)
    return tuple(finish(count, s, lat, pieces))


def solution(mesh):
    placed = (
        P("dp", None),
        P("dp", None),
        P("dp", "head"),
        P(None, "head"),
        P(None, "head"),
        P(None, "head"),
    )
    return jax.shard_map(
        per_device,
        mesh=mesh,
        in_specs=placed,
        out_specs=(
            P(("dp", "head"), None),
            P(("dp", "head"), None),
            P(None, "head"),
            P(None, "head"),
            P(None, "head"),
        ),
        check_vma=False,
    )
```

```python
import functools

import jax
import jax.numpy as jnp
import numpy as np
from jax import lax
from jax.experimental import pallas as pl
from jax.experimental.pallas import tpu as pltpu
from jax.sharding import PartitionSpec as P

QL = 1536
KL = 512
DN = 128
DR = 64
DQ = DN + DR
ROWS = 256
HEADS = 4
LAT = 2176

max_rms = 1.0
eps = 1e-06

MESH = pl.DeviceIdType.MESH
BF = jnp.bfloat16
F32 = jnp.float32

PAIRS = 2
QC = 2 * DQ
KC = 4 * DN
TURNS = ("XBA", "AXB", "BAX")
QUERY = tuple(
    (768 * c + 256 * u, 256, QC, ("AB", "BA")[c], TURNS[u]) for u in range(3) for c in range(2)
)
KEYVAL = tuple(
    (j, 256 * u, 256, KC, ("ABX", "BAX")[u], ("BAX", "ABX")[u]) for j in range(PAIRS) for u in range(2)
)
NQ, NK = len(QUERY), len(KEYVAL)
PIECES = QUERY + tuple(k[1:] for k in KEYVAL)
N = NQ + NK
STEP = 32


def tables():
    half = DR // 2
    freqs = np.float32(10000.0) ** (np.float32(-2.0) * np.arange(half, dtype=np.float32) / DR)
    angle = np.arange(ROWS, dtype=np.float32)[:, None] * freqs.astype(np.float32)[None, :]
    cosine, sine = np.cos(angle), np.sin(angle)
    swap = np.zeros((DR, DR), np.float32)
    for i in range(half):
        swap[half + i, i] = -1.0
        swap[i, half + i] = 1.0
    trig = np.concatenate([cosine, cosine, sine, sine], axis=1)
    return trig.astype(np.float32), swap


def for_rows(rows, step, body):
    def one(i, carry):
        body(pl.multiple_of(i * step, step))
        return carry

    lax.fori_loop(0, rows // step, one, 0)


def places():
    d, h = lax.axis_index("dp"), lax.axis_index("head")
    y, xh = d // 2, d % 2
    b, y0 = y // 2, y % 2
    a = (y0 + b) % 2
    z, r = h // 4, h % 4
    xl, c = r // 2, r % 2
    bits = {"A": a, "B": b, "X": xh}
    ya, yb, yab = y + 1 - 2 * y0, 3 - y, 2 - y + 2 * y0
    peer = {
        "A": (2 * ya + xh, h),
        "B": (2 * yb + xh, h),
        "X": (2 * y + 1 - xh, h),
        "AB": (2 * yab + xh, h),
        "AX": (2 * ya + 1 - xh, h),
        "BX": (2 * yb + 1 - xh, h),
        "ABX": (2 * yab + 1 - xh, h),
        "C": (d, h + 1 - 2 * c),
        "L": (d, h + 2 - 4 * xl),
    }
    for k in range(1, 8):
        peer["Z%d" % k] = (d, (h + 4 * k) % 32)
    return bits, peer, d, z, xl, c


def dot(left, right):
    return jnp.dot(left, right, preferred_element_type=F32)


def dot_nt(left, right):
    return lax.dot_general(left, right, (((1,), (1,)), ((), ())), preferred_element_type=F32)


def dot_tn(left, right):
    return lax.dot_general(left, right, (((0,), (0,)), ((), ())), preferred_element_type=F32)


def step_kernel(*refs):
    refs = list(refs)

    def take(n):
        out = refs[:n]
        del refs[:n]
        return out

    ql_hbm, kvl_hbm, dy_hbm, wq_hbm, wk_hbm, wv_hbm, trig_hbm, swap_hbm = take(8)
    g = take(N)
    s_out, lat_out = take(2)
    ql, kvlt, dy, wq, wk, wv, trig, swap, qx, qlt, dq_away, dqs, dkv = take(13)
    stg, rcv, ra, rb = take(N), take(N), take(N), take(N)
    lat, lrecv, lsum, zs, zr, lx, lxr, sq, sd, sl, slr, sc, scr, sf, sz = take(15)
    in_sem, rs_send, rs_recv, ag_send, ag_recv, q_send, q_recv, l_send, l_recv, s_send, s_recv = take(11)

    def pair(ref, j, width):
        return ref.at[:, pl.ds(width * j, width)]

    loads = [
        pltpu.make_async_copy(src, dst, in_sem.at[i])
        for i, (src, dst) in enumerate((
            (kvl_hbm, kvlt), (pair(wk_hbm, 0, 2 * DN), wk.at[0]), (pair(wk_hbm, 1, 2 * DN), wk.at[1]),
            (pair(wv_hbm, 0, 2 * DN), wv.at[0]), (pair(wv_hbm, 1, 2 * DN), wv.at[1]), (ql_hbm, ql),
            (trig_hbm, trig), (swap_hbm, swap), (pair(wq_hbm, 0, QC), wq.at[0]),
            (pair(wq_hbm, 1, QC), wq.at[1]), (pair(dy_hbm, 0, 2 * DN), dy.at[0]),
            (pair(dy_hbm, 1, 2 * DN), dy.at[1]),
        ))
    ]
    for load in loads:
        load.start()
    bits, peer, d, z, xl, c = places()
    barrier = pltpu.get_barrier_semaphore()
    for where in peer.values():
        pl.semaphore_signal(barrier, inc=1, device_id=where, device_id_type=MESH)

    def remote(src, dst, send, recv, where):
        copy = pltpu.make_async_remote_copy(
            src_ref=src, dst_ref=dst, send_sem=send, recv_sem=recv,
            device_id=peer[where], device_id_type=MESH,
        )
        copy.start()
        return copy

    def product(p, lo, n):
        r0 = PIECES[p][0]
        if p >= NQ:
            return dot(kvlt[pl.ds(r0 + lo, n), :], dkv[KEYVAL[p - NQ][0]])
        return dot(qlt[pl.ds(r0 + lo, n), :], dqs[...])

    def area(p, s):
        rows = PIECES[p][1]
        return (0, rows // 2, rows // 2 + rows // 4)[s], rows >> (s + 1)

    def bit(p, s):
        return bits[PIECES[p][3][s]]

    def rs_send_off(p, s):
        off, n = area(p, s)
        return remote(
            stg[p].at[pl.ds(off, n)], rcv[p].at[pl.ds(off, n)],
            rs_send.at[p, s], rs_recv.at[p, s], PIECES[p][3][s],
        )

    def rs_first(p):
        off, n = area(p, 0)
        away = pl.multiple_of((1 - bit(p, 0)) * n, 128)
        stg[p][:n, :] = product(p, away, n).astype(BF)
        return rs_send_off(p, 0)

    def rs_keep(p):
        off, n = area(p, 0)
        keep = pl.multiple_of(bit(p, 0) * n, 128)
        ra[p][...] = product(p, keep, n)

    def rs_second(p, copy):
        copy.wait()
        off, n = area(p, 1)
        away, keep = (1 - bit(p, 1)) * n, bit(p, 1) * n

        def total(lo):
            return ra[p][pl.ds(lo, STEP), :] + rcv[p][pl.ds(lo, STEP), :].astype(F32)

        def out(i):
            stg[p][pl.ds(off + i, STEP), :] = total(pl.multiple_of(away + i, 32)).astype(BF)

        for_rows(n, STEP, out)
        sent = rs_send_off(p, 1)

        def hold(i):
            rb[p][pl.ds(i, STEP), :] = total(pl.multiple_of(keep + i, 32))

        for_rows(n, STEP, hold)
        return sent

    def rs_third(p, copy):
        copy.wait()
        before, _ = area(p, 1)
        off, n = area(p, 2)
        away = (1 - bit(p, 2)) * n

        def out(i):
            lo = pl.multiple_of(away + i, 32)
            stg[p][pl.ds(off + i, STEP), :] = (
                rb[p][pl.ds(lo, STEP), :]
                + rcv[p][pl.ds(pl.multiple_of(before + lo, 32), STEP), :].astype(F32)
            ).astype(BF)

        for_rows(n, STEP, out)
        return rs_send_off(p, 2)

    def rs_last(p, copy):
        copy.wait()
        before, n = area(p, 1)
        if p >= NQ:
            off, n = area(p, 2)
            keep = bit(p, 2) * n
            place = (bit(p, 0), bit(p, 1), bit(p, 2))
        else:
            keep = 0
            place = (bits["X"], bit(p, 0), bit(p, 1))

        def body(i):
            at = pl.multiple_of(keep + i, 32)
            total = rb[p][pl.ds(at, STEP), :] + rcv[p][
                pl.ds(pl.multiple_of(before + at, 32), STEP), :
            ].astype(F32)
            if p >= NQ:
                total = total + rcv[p][pl.ds(off + i, STEP), :].astype(F32)
            g[p][place + (pl.ds(i, STEP), slice(None))] = total.astype(BF)
            square = total * total
            part = square[:, :128]
            for j in range(1, square.shape[1] // 128):
                part = part + square[:, 128 * j : 128 * (j + 1)]
            sq[...] = sq[...] + part[:8] + part[8:16] + part[16:24] + part[24:32]

        for_rows(n, STEP, body)

    def ag_start(p, s):
        order = PIECES[p][4]
        dims = PIECES[p][3] if p >= NQ else "X" + PIECES[p][3]
        where = tuple(
            pl.ds(0, 2) if name in order[:s] else pl.ds(bits[name], 1) for name in dims
        )
        block = g[p].at[where]
        return remote(block, block, ag_send.at[p, s], ag_recv.at[p, s], order[s])

    for load in loads[:5]:
        load.wait()
    plain = jnp.transpose(kvlt[:KL, :])
    key_rot = jnp.transpose(kvlt[KL:, :])
    scale = 1.0 / DQ**0.5
    allowed = lax.broadcasted_iota(jnp.int32, (ROWS, ROWS), 0) <= lax.broadcasted_iota(
        jnp.int32, (ROWS, ROWS), 1
    )
    rot = jnp.zeros((ROWS, DR), F32)
    loads[5].wait()
    pl.semaphore_wait(barrier, len(peer))
    half = pl.ds(pl.multiple_of(c * (QL // 2), 128), QL // 2)
    q_copy = remote(ql.at[:, half], qx.at[:, half], q_send.at[0], q_recv.at[0], "X")
    qlt[:, :ROWS] = jnp.transpose(ql[...])
    for load in loads[6:]:
        load.wait()
    cosine, sine = trig[:, :DR], trig[:, DR:]
    turn = swap[...]
    for t in range(PAIRS):
        j = bits["X"] if t else 1 - bits["X"]
        keys = dot(plain, wk[j]).astype(BF)
        values = dot(plain, wv[j]).astype(BF)
        queries = dot(ql[...], wq[j]).astype(BF)
        parts = []
        for n in range(2):
            q_plain = queries[:, DQ * n : DQ * n + DN]
            q_rot = queries[:, DQ * n + DN : DQ * (n + 1)]
            q_rope = (q_rot.astype(F32) * cosine + dot(q_rot, turn) * sine).astype(BF)
            key = keys[:, DN * n : DN * (n + 1)]
            value = values[:, DN * n : DN * (n + 1)]
            grad = dy[j, :, DN * n : DN * (n + 1)]
            q_all = jnp.concatenate([q_plain, q_rope], axis=1)
            k_all = jnp.concatenate([key, key_rot], axis=1)
            scores = jnp.where(allowed, dot_nt(k_all, q_all) * scale, -jnp.inf)
            top = jnp.max(scores, axis=0, keepdims=True)
            weights = jnp.exp(scores - top)
            probs = weights / jnp.sum(weights, axis=0, keepdims=True)
            dkv[j, :, 2 * DN + DN * n : 2 * DN + DN * (n + 1)] = dot(
                probs.astype(BF), grad
            ).astype(BF)
            dp = dot_nt(value, grad)
            mean = jnp.sum(dp * probs, axis=0, keepdims=True)
            ds = (probs * (dp - mean) * scale).astype(BF)
            dk = dot(ds, q_all)
            dkv[j, :, DN * n : DN * (n + 1)] = dk[:, :DN].astype(BF)
            rot = rot + dk[:, DN:].astype(BF).astype(F32)
            dq = dot_tn(ds, k_all)
            d_rope = dq[:, DN:].astype(BF)
            d_rot = d_rope.astype(F32) * cosine + dot_nt(d_rope, turn) * sine
            parts.append(jnp.concatenate([dq[:, :DN].astype(BF), d_rot.astype(BF)], axis=1))
        if t == 0:
            dq_away[...] = jnp.concatenate(parts, axis=1)
            d_copy = remote(
                dq_away, dqs.at[pl.ds(ROWS, ROWS)], q_send.at[1], q_recv.at[1], "X"
            )
        else:
            dqs[:ROWS, :] = jnp.concatenate(parts, axis=1)
    keyval = range(NQ, N)
    moving = [None] * N
    for p in keyval:
        moving[p] = rs_first(p)

    own = bits["X"]
    lat[:, :, :, :QL] = (dot_nt(dq_away[...], wq[1 - own]) + dot_nt(dqs[:ROWS, :], wq[own])).reshape(
        16, 2, 8, QL
    )
    term = dot_nt(dkv[0, :, : 2 * DN], wk[0]) + dot_nt(dkv[1, :, : 2 * DN], wk[1])
    term = term + dot_nt(dkv[0, :, 2 * DN :], wv[0]) + dot_nt(dkv[1, :, 2 * DN :], wv[1])
    lat[:, :, :, QL : QL + KL] = term.reshape(16, 2, 8, KL)
    lat[:, :, :, QL + KL :] = jnp.concatenate([rot, jnp.zeros((ROWS, DR), F32)], axis=1).reshape(
        16, 2, 8, 128
    )
    core = remote(lat.at[:, 1 - c], lrecv, l_send.at[0], l_recv.at[0], "C")
    for p in keyval:
        rs_keep(p)
    q_copy.wait()
    forward = remote(qx.at[:, half], qx.at[:, half], q_send.at[2], q_recv.at[2], "C")
    core.wait()

    def core_body(k, carry):
        lsum[k] = lat[k, c] + lrecv[k]
        return carry

    lax.fori_loop(0, 16, core_body, 0)

    def zs_body(k, carry):
        zs[k] = jnp.concatenate([lsum[2 * k], lsum[2 * k + 1]], axis=0).astype(BF)
        return carry

    lax.fori_loop(0, 8, zs_body, 0)
    zcopies = [
        remote(zs.at[(z + k) % 8], zr.at[k - 1], l_send.at[k], l_recv.at[k], "Z%d" % k)
        for k in range(1, 8)
    ]
    forward.wait()
    qlt[:, ROWS:] = jnp.transpose(qx[...])
    for p in keyval[:2]:
        moving[p] = rs_second(p, moving[p])
    d_copy.wait()
    for p in range(NQ):
        moving[p] = rs_first(p)
    for p in keyval[2:]:
        moving[p] = rs_second(p, moving[p])
    for p in range(NQ):
        rs_keep(p)
    for p in keyval:
        moving[p] = rs_third(p, moving[p])
    sq[...] = jnp.zeros((8, 128), F32)
    for p in keyval:
        rs_last(p, moving[p])
        moving[p] = ag_start(p, 0)
    for p in range(NQ):
        moving[p] = rs_second(p, moving[p])
    for p in keyval:
        moving[p].wait()
        moving[p] = ag_start(p, 1)
    for p in range(NQ):
        rs_last(p, moving[p])
        moving[p] = ag_start(p, 0)

    cube = [
        remote(sq, sd.at[d], s_send.at[i], s_recv.at[i], where)
        for i, where in enumerate(("A", "B", "X", "AB", "AX", "BX", "ABX"))
    ]
    sd[d] = sq[...]
    for p in keyval:
        moving[p].wait()
        moving[p] = ag_start(p, 2)
    for p in range(NQ):
        moving[p].wait()
        moving[p] = ag_start(p, 1)
    for copy in cube:
        copy.wait()
    total = sd[0]
    for i in range(1, 8):
        total = total + sd[i]
    sl[...] = total
    ls = remote(sl, slr, s_send.at[7], s_recv.at[7], "L")
    for copy in zcopies:
        copy.wait()
    lx[0] = lsum[2 * z]
    lx[1] = lsum[2 * z + 1]
    for k in range(7):
        got = zr[k].astype(F32)
        lx[0] = lx[0] + got[:8]
        lx[1] = lx[1] + got[8:]
    xcopy = remote(lx.at[1 - xl], lxr, l_send.at[8], l_recv.at[8], "L")
    for p in range(NQ):
        moving[p].wait()
        moving[p] = ag_start(p, 2)
    ls.wait()
    sc[...] = sl[...] + slr[...]
    cs = remote(sc, scr, s_send.at[8], s_recv.at[8], "C")
    xcopy.wait()
    lat_out[...] = lx[xl] + lxr[...]
    cs.wait()
    sf[...] = sc[...] + scr[...]
    zsum = [
        remote(sf, sz.at[z], s_send.at[8 + k], s_recv.at[8 + k], "Z%d" % k) for k in range(1, 8)
    ]
    sz[z] = sf[...]
    for copy in zsum:
        copy.wait()
    s_out[...] = sz[...]
    for copy in moving:
        copy.wait()


def gathered(p):
    return (2, 2, 2, PIECES[p][1] // (8 if p >= NQ else 4), PIECES[p][2])


def step(ql, kvl, dy, wq, wk, wv):
    trig, swap = tables()
    vmem = pl.BlockSpec(memory_space=pltpu.VMEM)
    hbm = pl.BlockSpec(memory_space=pltpu.HBM)

    def buffer(p, part, dtype):
        return pltpu.VMEM((PIECES[p][1] * part // 8, PIECES[p][2]), dtype)

    scratch = [
        pltpu.VMEM((ROWS, QL), BF),
        pltpu.VMEM((KL + DR, ROWS), BF),
        pltpu.VMEM((PAIRS, ROWS, 2 * DN), BF),
        pltpu.VMEM((PAIRS, QL, QC), BF),
        pltpu.VMEM((PAIRS, KL, 2 * DN), BF),
        pltpu.VMEM((PAIRS, KL, 2 * DN), BF),
        pltpu.VMEM((ROWS, 2 * DR), F32),
        pltpu.VMEM((DR, DR), BF),
        pltpu.VMEM((ROWS, QL), BF),
        pltpu.VMEM((QL, 2 * ROWS), BF),
        pltpu.VMEM((ROWS, QC), BF),
        pltpu.VMEM((2 * ROWS, QC), BF),
        pltpu.VMEM((PAIRS, ROWS, KC), BF),
    ]
    scratch += [buffer(p, 7 if p >= NQ else 6, BF) for p in range(N)] * 2
    scratch += [buffer(p, 4, F32) for p in range(N)]
    scratch += [buffer(p, 2, F32) for p in range(N)]
    tile = (8, 128)
    scratch += [
        pltpu.VMEM((16, 2, 8, LAT), F32),
        pltpu.VMEM((16, 8, LAT), F32),
        pltpu.VMEM((16, 8, LAT), F32),
        pltpu.VMEM((8, 16, LAT), BF),
        pltpu.VMEM((7, 16, LAT), BF),
        pltpu.VMEM((2, 8, LAT), F32),
        pltpu.VMEM((8, LAT), F32),
        pltpu.VMEM(tile, F32),
        pltpu.VMEM((8,) + tile, F32),
    ]
    scratch += [pltpu.VMEM(tile, F32)] * 5 + [pltpu.VMEM((8,) + tile, F32)]
    dma = pltpu.SemaphoreType.DMA
    scratch += [dma((12,)), dma((N, 3)), dma((N, 3)), dma((N, 3)), dma((N, 3))]
    scratch += [dma((3,)), dma((3,)), dma((9,)), dma((9,)), dma((16,)), dma((16,))]
    args = (ql, kvl, dy, wq, wk, wv, jnp.asarray(trig), jnp.asarray(swap, BF))
    return pl.pallas_call(
        step_kernel,
        out_shape=tuple(jax.ShapeDtypeStruct(gathered(p), BF) for p in range(N))
        + (jax.ShapeDtypeStruct((8, 8, 128), F32), jax.ShapeDtypeStruct((8, LAT), F32)),
        in_specs=[hbm] * 8,
        out_specs=(vmem,) * (N + 2),
        scratch_shapes=scratch,
        name="step",
        compiler_params=pltpu.CompilerParams(
            collective_id=0, has_side_effects=True, vmem_limit_bytes=46 << 20
        ),
    )(*(pltpu.with_memory_space_constraint(t, pltpu.HBM) for t in args))


def finish_kernel(count, *refs):
    s_ref, lat_ref = refs[:2]
    g = refs[2 : 2 + N]
    ql_out, kvl_out, q_out, k_out, v_out = refs[2 + N : 7 + N]
    buffers = refs[7 + N : 7 + 2 * N]
    kvl, sem = refs[7 + 2 * N :]
    kvl[...] = lat_ref[:, QL : QL + KL + DR]
    copies = []

    def start(src, dst):
        copy = pltpu.make_async_copy(src, dst, sem.at[len(copies)])
        copy.start()
        copies.append(copy)

    start(lat_ref.at[:, pl.ds(0, QL)], ql_out)
    start(kvl, kvl_out)
    total = jnp.sum(s_ref[...], axis=0)
    total = jnp.sum(total, axis=0, keepdims=True)
    total = jnp.sum(total, axis=1, keepdims=True)
    factor = jnp.minimum(1.0, max_rms * count**0.5 / jnp.sqrt(total + eps))
    for p in range(N):
        r0, rows = PIECES[p][:2]
        for a in range(2):

            def body(i, carry):
                one, two = i // 2, i % 2
                buffers[p][a, one, two] = (g[p][a, one, two].astype(F32) * factor).astype(BF)
                return carry

            lax.fori_loop(0, 4, body, 0)
            if p < NQ:
                for one in range(2):
                    for two in range(2):
                        n = rows // 4
                        start(
                            buffers[p].at[a, one, two],
                            q_out.at[pl.ds(r0 + n * (2 * one + two), n), pl.ds(QC * a, QC)],
                        )
            else:
                pair = KEYVAL[p - NQ][0]
                half = pl.ds(2 * DN * pair, 2 * DN)
                n = rows // 8
                for one in range(2):
                    for two in range(2):
                        at = pl.ds(r0 + n * (4 * a + 2 * one + two), n)
                        block = buffers[p].at[a, one, two]
                        start(block.at[:, pl.ds(0, 2 * DN)], k_out.at[at, half])
                        start(block.at[:, pl.ds(2 * DN, 2 * DN)], v_out.at[at, half])
    for copy in copies:
        copy.wait()


def finish(count, s, lat, pieces):
    vmem = pl.BlockSpec(memory_space=pltpu.VMEM)
    hbm = pl.BlockSpec(memory_space=pl.ANY)
    return pl.pallas_call(
        functools.partial(finish_kernel, count),
        out_shape=(
            jax.ShapeDtypeStruct((8, QL), F32),
            jax.ShapeDtypeStruct((8, KL + DR), F32),
            jax.ShapeDtypeStruct((QL, HEADS * DQ), BF),
            jax.ShapeDtypeStruct((KL, HEADS * DN), BF),
            jax.ShapeDtypeStruct((KL, HEADS * DN), BF),
        ),
        in_specs=[vmem] * (N + 2),
        out_specs=(hbm,) * 5,
        scratch_shapes=[pltpu.VMEM(gathered(p), BF) for p in range(N)]
        + [pltpu.VMEM((8, KL + DR), F32), pltpu.SemaphoreType.DMA((2 + 8 * NQ + 16 * NK,))],
        name="finish",
        compiler_params=pltpu.CompilerParams(vmem_limit_bytes=16 << 20),
    )(s, lat, *pieces)


def per_device(query_latent, kv_latent, out_grad, query_up, key_up, value_up):
    width = lax.axis_size("head")
    count = (QL * query_up.shape[1] + 2 * KL * key_up.shape[1]) * width
    *pieces, s, lat = step(query_latent, kv_latent.T, out_grad, query_up, key_up, value_up)
    return tuple(finish(count, s, lat, pieces))


def solution(mesh):
    placed = (
        P("dp", None),
        P("dp", None),
        P("dp", "head"),
        P(None, "head"),
        P(None, "head"),
        P(None, "head"),
    )
    return jax.shard_map(
        per_device,
        mesh=mesh,
        in_specs=placed,
        out_specs=(
            P(("dp", "head"), None),
            P(("dp", "head"), None),
            P(None, "head"),
            P(None, "head"),
            P(None, "head"),
        ),
        check_vma=False,
    )
```

```python
import functools

import jax
import jax.numpy as jnp
import numpy as np
from jax import lax
from jax.experimental import pallas as pl
from jax.experimental.pallas import tpu as pltpu
from jax.sharding import PartitionSpec as P

QL = 1536
KL = 512
DN = 128
DR = 64
DQ = DN + DR
ROWS = 256
HEADS = 4
LAT = 2176

max_rms = 1.0
eps = 1e-06

MESH = pl.DeviceIdType.MESH
BF = jnp.bfloat16
F32 = jnp.float32

PAIRS = 2
QC = 2 * DQ
KC = 4 * DN
SHAPES = ((768, QC), (768, QC), (512, KC))
G = PAIRS * len(SHAPES)
ORDERS = ("ABX", "BXA", "XAB")
SUBS = (2, 2, 2)
PIECES = tuple(
    (3 * j + kind, kind, SHAPES[kind][0] // SUBS[kind] * u, SHAPES[kind][0] // SUBS[kind])
    for j in range(PAIRS)
    for u in range(max(SUBS))
    for kind in range(3)
    if u < SUBS[kind]
)
N = len(PIECES)
CUTS = 2
STEPS = (48, 48, 32)


def tables():
    half = DR // 2
    freqs = np.float32(10000.0) ** (np.float32(-2.0) * np.arange(half, dtype=np.float32) / DR)
    angle = np.arange(ROWS, dtype=np.float32)[:, None] * freqs.astype(np.float32)[None, :]
    cosine, sine = np.cos(angle), np.sin(angle)
    swap = np.zeros((DR, DR), np.float32)
    for i in range(half):
        swap[half + i, i] = -1.0
        swap[i, half + i] = 1.0
    trig = np.stack([np.concatenate([t, t], axis=1) for t in (cosine, sine)])
    return trig.astype(np.float32), swap


def for_rows(rows, step, body):
    def one(i, carry):
        body(pl.multiple_of(i * step, step))
        return carry

    lax.fori_loop(0, rows // step, one, 0)


def places():
    d, h = lax.axis_index("dp"), lax.axis_index("head")
    y, xh = d // 2, d % 2
    b, y0 = y // 2, y % 2
    a = (y0 + b) % 2
    z, r = h // 4, h % 4
    xl, c = r // 2, r % 2
    bits = {"A": a, "B": b, "X": xh}
    ya, yb, yab = y + 1 - 2 * y0, 3 - y, 2 - y + 2 * y0
    peer = {
        "A": (2 * ya + xh, h),
        "B": (2 * yb + xh, h),
        "X": (2 * y + 1 - xh, h),
        "AB": (2 * yab + xh, h),
        "AX": (2 * ya + 1 - xh, h),
        "BX": (2 * yb + 1 - xh, h),
        "ABX": (2 * yab + 1 - xh, h),
        "C": (d, h + 1 - 2 * c),
        "L": (d, h + 2 - 4 * xl),
    }
    for k in range(1, 8):
        peer["Z%d" % k] = (d, (h + 4 * k) % 32)
    return bits, peer, d, z, xl, c


def dot(left, right):
    return jnp.dot(left, right, preferred_element_type=F32)


def dot_nt(left, right):
    return lax.dot_general(left, right, (((1,), (1,)), ((), ())), preferred_element_type=F32)


def dot_tn(left, right):
    return lax.dot_general(left, right, (((0,), (0,)), ((), ())), preferred_element_type=F32)


def step_kernel(*refs):
    refs = list(refs)

    def take(n):
        out = refs[:n]
        del refs[:n]
        return out

    ql_hbm, kvl_hbm, dy_hbm, wq_hbm, wk_hbm, wv_hbm, trig_hbm, swap_hbm = take(8)
    g = take(G)
    s_out, lat_out = take(2)
    ql, kvlt, dy, wq, wk, wv, trig, swap, qlt, dqs, dkv = take(11)
    stg, rcv, ra, rb = take(N), take(N), take(N), take(N)
    lat, lrecv, lsum, zs, zr, lx, lxr, sq, sd, sl, slr, sc, scr, sf, sz = take(15)
    in_sem, rs_send, rs_recv, ag_send, ag_recv, l_send, l_recv, s_send, s_recv = take(9)

    loads = [
        pltpu.make_async_copy(src, dst, in_sem.at[i])
        for i, (src, dst) in enumerate((
            (kvl_hbm, kvlt), (wk_hbm, wk), (wv_hbm, wv), (ql_hbm, ql),
            (wq_hbm.at[:, pl.ds(0, QC)], wq.at[0]), (dy_hbm, dy), (trig_hbm, trig), (swap_hbm, swap),
            (wq_hbm.at[:, pl.ds(QC, QC)], wq.at[1]),
        ))
    ]
    for load in loads:
        load.start()
    bits, peer, d, z, xl, c = places()
    barrier = pltpu.get_barrier_semaphore()
    for where in peer.values():
        pl.semaphore_signal(barrier, inc=1, device_id=where, device_id_type=MESH)

    def remote(src, dst, send, recv, where):
        copy = pltpu.make_async_remote_copy(
            src_ref=src, dst_ref=dst, send_sem=send, recv_sem=recv,
            device_id=peer[where], device_id_type=MESH,
        )
        copy.start()
        return copy

    def cut(p):
        return PIECES[p][1], PIECES[p][3], STEPS[PIECES[p][1]]

    def product(p, lo, n):
        array, kind, r0, _ = PIECES[p]
        if kind == 2:
            return dot(kvlt[pl.ds(r0 + lo, n), :], dkv[array // 3])
        return dot(qlt[pl.ds(768 * kind + r0 + lo, n), :], dqs[array // 3])

    def area(p, s):
        rows = cut(p)[1]
        return (0, rows // 2, rows // 2 + rows // 4)[s], rows >> (s + 1)

    def dim(p, s):
        return ORDERS[cut(p)[0]][s]

    def rs_send_off(p, s):
        off, n = area(p, s)
        return remote(
            stg[p].at[pl.ds(off, n)], rcv[p].at[pl.ds(off, n)],
            rs_send.at[p, s], rs_recv.at[p, s], dim(p, s),
        )

    def rs_first(p):
        off, n = area(p, 0)
        away = pl.multiple_of((1 - bits[dim(p, 0)]) * n, 64)
        stg[p][:n, :] = product(p, away, n).astype(BF)
        return rs_send_off(p, 0)

    def rs_keep(p):
        off, n = area(p, 0)
        keep = pl.multiple_of(bits[dim(p, 0)] * n, 64)
        ra[p][...] = product(p, keep, n)

    def rs_second(p, copy):
        copy.wait()
        off, n = area(p, 1)
        bit = bits[dim(p, 1)]
        away, keep = (1 - bit) * n, bit * n
        rows = cut(p)[2]

        def total(lo):
            return ra[p][pl.ds(lo, rows), :] + rcv[p][pl.ds(lo, rows), :].astype(F32)

        def out(i):
            stg[p][pl.ds(off + i, rows), :] = total(pl.multiple_of(away + i, 16)).astype(BF)

        for_rows(n, rows, out)
        sent = rs_send_off(p, 1)

        def hold(i):
            rb[p][pl.ds(i, rows), :] = total(pl.multiple_of(keep + i, 16))

        for_rows(n, rows, hold)
        return sent

    def rs_third(p, copy):
        copy.wait()
        before, _ = area(p, 1)
        off, n = area(p, 2)
        away = (1 - bits[dim(p, 2)]) * n
        rows = cut(p)[2]

        def out(i):
            lo = pl.multiple_of(away + i, 16)
            stg[p][pl.ds(off + i, rows), :] = (
                rb[p][pl.ds(lo, rows), :]
                + rcv[p][pl.ds(pl.multiple_of(before + lo, 16), rows), :].astype(F32)
            ).astype(BF)

        for_rows(n, rows, out)
        return rs_send_off(p, 2)

    def owned(p, s):
        lo = PIECES[p][2]
        for t in range(s + 1):
            lo = lo + bits[dim(p, t)] * (cut(p)[1] >> (t + 1))
        return pl.multiple_of(lo, 16)

    def rs_last(p, copy):
        copy.wait()
        before, _ = area(p, 1)
        off, n = area(p, 2)
        keep = bits[dim(p, 2)] * n
        lo = owned(p, 2)
        rows = cut(p)[2]
        out = g[PIECES[p][0]]

        def body(i):
            at = pl.multiple_of(keep + i, 16)
            total = (
                rb[p][pl.ds(at, rows), :]
                + rcv[p][pl.ds(pl.multiple_of(before + at, 16), rows), :].astype(F32)
                + rcv[p][pl.ds(off + i, rows), :].astype(F32)
            )
            out[pl.ds(pl.multiple_of(lo + i, 16), rows), :] = total.astype(BF)
            square = total * total
            part = square[:, :128]
            for j in range(1, square.shape[1] // 128):
                part = part + square[:, 128 * j : 128 * (j + 1)]
            left = sq[...]
            for j in range(0, rows, 8):
                left = left + part[j : j + 8]
            sq[...] = left

        for_rows(n, rows, body)

    def ag_start(p, s):
        block = g[PIECES[p][0]].at[pl.ds(owned(p, s), cut(p)[1] >> (s + 1))]
        return remote(block, block, ag_send.at[p, s], ag_recv.at[p, s], dim(p, s))

    for load in loads[:3]:
        load.wait()
    plain = jnp.transpose(kvlt[:KL, :])
    key_rot = jnp.transpose(kvlt[KL:, :])
    scale = 1.0 / DQ**0.5
    allowed = lax.broadcasted_iota(jnp.int32, (ROWS, ROWS), 0) <= lax.broadcasted_iota(
        jnp.int32, (ROWS, ROWS), 1
    )
    rot = jnp.zeros((ROWS, DR), F32)
    moving = []
    for j in range(PAIRS):
        cols = slice(2 * DN * j, 2 * DN * (j + 1))
        keys = dot(plain, wk[:, cols]).astype(BF)
        values = dot(plain, wv[:, cols]).astype(BF)
        if j == 0:
            for load in loads[3:8]:
                load.wait()
            cosine, sine = trig[0], trig[1]
            turn = swap[...]
        else:
            loads[8].wait()
        queries = dot(ql[...], wq[j]).astype(BF)
        if j == 0:
            qlt[...] = jnp.transpose(ql[...])
        parts = []
        for n in range(2):
            q_plain = queries[:, DQ * n : DQ * n + DN]
            q_rot = queries[:, DQ * n + DN : DQ * (n + 1)]
            q_rope = (q_rot.astype(F32) * cosine + dot(q_rot, turn) * sine).astype(BF)
            key = keys[:, DN * n : DN * (n + 1)]
            value = values[:, DN * n : DN * (n + 1)]
            grad = dy[:, 2 * DN * j + DN * n : 2 * DN * j + DN * (n + 1)]
            q_all = jnp.concatenate([q_plain, q_rope], axis=1)
            k_all = jnp.concatenate([key, key_rot], axis=1)
            scores = jnp.where(allowed, dot_nt(k_all, q_all) * scale, -jnp.inf)
            top = jnp.max(scores, axis=0, keepdims=True)
            weights = jnp.exp(scores - top)
            probs = weights / jnp.sum(weights, axis=0, keepdims=True)
            dkv[j, :, 2 * DN + DN * n : 2 * DN + DN * (n + 1)] = dot(
                probs.astype(BF), grad
            ).astype(BF)
            dp = dot_nt(value, grad)
            mean = jnp.sum(dp * probs, axis=0, keepdims=True)
            ds = (probs * (dp - mean) * scale).astype(BF)
            dk = dot(ds, q_all)
            dkv[j, :, DN * n : DN * (n + 1)] = dk[:, :DN].astype(BF)
            rot = rot + dk[:, DN:].astype(BF).astype(F32)
            dq = dot_tn(ds, k_all)
            d_rope = dq[:, DN:].astype(BF)
            d_rot = d_rope.astype(F32) * cosine + dot_nt(d_rope, turn) * sine
            parts.append(jnp.concatenate([dq[:, :DN].astype(BF), d_rot.astype(BF)], axis=1))
        dqs[j] = jnp.concatenate(parts, axis=1)
        if j == 0:
            pl.semaphore_wait(barrier, len(peer))
        for p in range(N // PAIRS):
            moving.append(rs_first(N // PAIRS * j + p))

    lat[:, :, :, :QL] = (dot_nt(dqs[0], wq[0]) + dot_nt(dqs[1], wq[1])).reshape(16, 2, 8, QL)
    term = dot_nt(dkv[0, :, : 2 * DN], wk[:, : 2 * DN]) + dot_nt(dkv[1, :, : 2 * DN], wk[:, 2 * DN :])
    term = term + dot_nt(dkv[0, :, 2 * DN :], wv[:, : 2 * DN])
    term = term + dot_nt(dkv[1, :, 2 * DN :], wv[:, 2 * DN :])
    lat[:, :, :, QL : QL + KL] = term.reshape(16, 2, 8, KL)
    lat[:, :, :, QL + KL :] = jnp.concatenate([rot, jnp.zeros((ROWS, DR), F32)], axis=1).reshape(
        16, 2, 8, 128
    )
    core = remote(lat.at[:, 1 - c], lrecv, l_send.at[0], l_recv.at[0], "C")
    turns = list(range(N))
    for p in turns:
        rs_keep(p)
    for p in turns[:3]:
        moving[p] = rs_second(p, moving[p])
    core.wait()

    def core_body(k, carry):
        lsum[k] = lat[k, c] + lrecv[k]
        return carry

    lax.fori_loop(0, 16, core_body, 0)

    def zs_body(k, carry):
        zs[k] = jnp.concatenate([lsum[2 * k], lsum[2 * k + 1]], axis=0).astype(BF)
        return carry

    lax.fori_loop(0, 8, zs_body, 0)
    zcopies = [
        remote(zs.at[(z + k) % 8], zr.at[k - 1], l_send.at[k], l_recv.at[k], "Z%d" % k)
        for k in range(1, 8)
    ]
    for p in turns[3:]:
        moving[p] = rs_second(p, moving[p])
    for p in turns:
        moving[p] = rs_third(p, moving[p])
    sq[...] = jnp.zeros((8, 128), F32)
    for p in turns:
        rs_last(p, moving[p])
        moving[p] = ag_start(p, 2)

    cube = [
        remote(sq, sd.at[d], s_send.at[i], s_recv.at[i], where)
        for i, where in enumerate(("A", "B", "X", "AB", "AX", "BX", "ABX"))
    ]
    sd[d] = sq[...]
    for p in turns:
        moving[p].wait()
        moving[p] = ag_start(p, 1)
    for copy in cube:
        copy.wait()
    total = sd[0]
    for i in range(1, 8):
        total = total + sd[i]
    sl[...] = total
    ls = remote(sl, slr, s_send.at[7], s_recv.at[7], "L")
    for copy in zcopies:
        copy.wait()
    lx[0] = lsum[2 * z]
    lx[1] = lsum[2 * z + 1]
    for k in range(7):
        got = zr[k].astype(F32)
        lx[0] = lx[0] + got[:8]
        lx[1] = lx[1] + got[8:]
    xcopy = remote(lx.at[1 - xl], lxr, l_send.at[8], l_recv.at[8], "L")
    for p in turns:
        moving[p].wait()
        moving[p] = ag_start(p, 0)
    ls.wait()
    sc[...] = sl[...] + slr[...]
    cs = remote(sc, scr, s_send.at[8], s_recv.at[8], "C")
    xcopy.wait()
    lat_out[...] = lx[xl] + lxr[...]
    cs.wait()
    sf[...] = sc[...] + scr[...]
    zsum = [
        remote(sf, sz.at[z], s_send.at[8 + k], s_recv.at[8 + k], "Z%d" % k) for k in range(1, 8)
    ]
    sz[z] = sf[...]
    for copy in zsum:
        copy.wait()
    s_out[...] = sz[...]
    for copy in moving:
        copy.wait()


def step(ql, kvl, dy, wq, wk, wv):
    trig, swap = tables()
    vmem = pl.BlockSpec(memory_space=pltpu.VMEM)
    hbm = pl.BlockSpec(memory_space=pltpu.HBM)

    def buffer(p, rows, dtype):
        return pltpu.VMEM((rows, SHAPES[PIECES[p][1]][1]), dtype)

    scratch = [
        pltpu.VMEM((ROWS, QL), BF),
        pltpu.VMEM((KL + DR, ROWS), BF),
        pltpu.VMEM((ROWS, HEADS * DN), BF),
        pltpu.VMEM((PAIRS, QL, QC), BF),
        pltpu.VMEM((KL, HEADS * DN), BF),
        pltpu.VMEM((KL, HEADS * DN), BF),
        pltpu.VMEM((2, ROWS, DR), F32),
        pltpu.VMEM((DR, DR), BF),
        pltpu.VMEM((QL, ROWS), BF),
        pltpu.VMEM((PAIRS, ROWS, QC), BF),
        pltpu.VMEM((PAIRS, ROWS, KC), BF),
    ]
    scratch += [buffer(p, PIECES[p][3] * 7 // 8, BF) for p in range(N)] * 2
    scratch += [buffer(p, PIECES[p][3] // 2, F32) for p in range(N)]
    scratch += [buffer(p, PIECES[p][3] // 4, F32) for p in range(N)]
    tile = (8, 128)
    scratch += [
        pltpu.VMEM((16, 2, 8, LAT), F32),
        pltpu.VMEM((16, 8, LAT), F32),
        pltpu.VMEM((16, 8, LAT), F32),
        pltpu.VMEM((8, 16, LAT), BF),
        pltpu.VMEM((7, 16, LAT), BF),
        pltpu.VMEM((2, 8, LAT), F32),
        pltpu.VMEM((8, LAT), F32),
        pltpu.VMEM(tile, F32),
        pltpu.VMEM((8,) + tile, F32),
    ]
    scratch += [pltpu.VMEM(tile, F32)] * 5 + [pltpu.VMEM((8,) + tile, F32)]
    dma = pltpu.SemaphoreType.DMA
    scratch += [dma((9,)), dma((N, 3)), dma((N, 3)), dma((N, 3)), dma((N, 3))]
    scratch += [dma((9,)), dma((9,)), dma((16,)), dma((16,))]
    args = (ql, kvl, dy, wq, wk, wv, jnp.asarray(trig), jnp.asarray(swap, BF))
    return pl.pallas_call(
        step_kernel,
        out_shape=tuple(jax.ShapeDtypeStruct(SHAPES[i % 3], BF) for i in range(G))
        + (jax.ShapeDtypeStruct((8, 8, 128), F32), jax.ShapeDtypeStruct((8, LAT), F32)),
        in_specs=[hbm] * 8,
        out_specs=(vmem,) * (G + 2),
        scratch_shapes=scratch,
        name="step",
        compiler_params=pltpu.CompilerParams(
            collective_id=0, has_side_effects=True, vmem_limit_bytes=46 << 20
        ),
    )(*(pltpu.with_memory_space_constraint(t, pltpu.HBM) for t in args))


def finish_kernel(count, *refs):
    s_ref, lat_ref = refs[:2]
    g = refs[2 : 2 + G]
    ql_out, kvl_out, q_out, k_out, v_out = refs[2 + G : 7 + G]
    buffers = refs[7 + G : 7 + 2 * G]
    kvl, sem = refs[7 + 2 * G :]
    kvl[...] = lat_ref[:, QL : QL + KL + DR]
    copies = []

    def start(src, dst):
        copy = pltpu.make_async_copy(src, dst, sem.at[len(copies)])
        copy.start()
        copies.append(copy)

    start(lat_ref.at[:, pl.ds(0, QL)], ql_out)
    start(kvl, kvl_out)
    total = jnp.sum(s_ref[...], axis=0)
    total = jnp.sum(total, axis=0, keepdims=True)
    total = jnp.sum(total, axis=1, keepdims=True)
    factor = jnp.minimum(1.0, max_rms * count**0.5 / jnp.sqrt(total + eps))
    for i in range(G):
        j, kind = i // 3, i % 3
        rows = SHAPES[kind][0] // CUTS
        for u in range(CUTS):
            at = pl.ds(rows * u, rows)

            for lo in range(0, rows, 64):
                where = slice(rows * u + lo, rows * u + lo + 64)
                buffers[i][where, :] = (g[i][where, :].astype(F32) * factor).astype(BF)

            if kind == 2:
                half = pl.ds(2 * DN * j, 2 * DN)
                start(buffers[i].at[at, pl.ds(0, 2 * DN)], k_out.at[at, half])
                start(buffers[i].at[at, pl.ds(2 * DN, 2 * DN)], v_out.at[at, half])
            else:
                start(
                    buffers[i].at[at],
                    q_out.at[pl.ds(768 * kind + rows * u, rows), pl.ds(QC * j, QC)],
                )
    for copy in copies:
        copy.wait()


def finish(count, s, lat, pieces):
    vmem = pl.BlockSpec(memory_space=pltpu.VMEM)
    hbm = pl.BlockSpec(memory_space=pl.ANY)
    return pl.pallas_call(
        functools.partial(finish_kernel, count),
        out_shape=(
            jax.ShapeDtypeStruct((8, QL), F32),
            jax.ShapeDtypeStruct((8, KL + DR), F32),
            jax.ShapeDtypeStruct((QL, HEADS * DQ), BF),
            jax.ShapeDtypeStruct((KL, HEADS * DN), BF),
            jax.ShapeDtypeStruct((KL, HEADS * DN), BF),
        ),
        in_specs=[vmem] * (G + 2),
        out_specs=(hbm,) * 5,
        scratch_shapes=[pltpu.VMEM(SHAPES[i % 3], BF) for i in range(G)]
        + [pltpu.VMEM((8, KL + DR), F32), pltpu.SemaphoreType.DMA((2 + CUTS * PAIRS * 4,))],
        name="finish",
        compiler_params=pltpu.CompilerParams(vmem_limit_bytes=16 << 20),
    )(s, lat, *pieces)


def per_device(query_latent, kv_latent, out_grad, query_up, key_up, value_up):
    width = lax.axis_size("head")
    count = (QL * query_up.shape[1] + 2 * KL * key_up.shape[1]) * width
    *pieces, s, lat = step(query_latent, kv_latent.T, out_grad, query_up, key_up, value_up)
    return tuple(finish(count, s, lat, pieces))


def solution(mesh):
    placed = (
        P("dp", None),
        P("dp", None),
        P("dp", "head"),
        P(None, "head"),
        P(None, "head"),
        P(None, "head"),
    )
    return jax.shard_map(
        per_device,
        mesh=mesh,
        in_specs=placed,
        out_specs=(
            P(("dp", "head"), None),
            P(("dp", "head"), None),
            P(None, "head"),
            P(None, "head"),
            P(None, "head"),
        ),
        check_vma=False,
    )
```
